512 devices in a mesh: chan: 64 (over y_lo, z, core), loc: 8 (over y_hi, x).
Axes of the slice: x: 4, y: 4 (y_hi: 2, y_lo: 2; y = y_hi * 2 + y_lo), z: 16, core: 2. Of those that a mesh axis runs over, the one named last changes fastest.
Arguments:
- pixels: bfloat16 [2048, 256, 256], P('loc', 'chan'), may hold values from -6 to 6
- patch_mask: int32 [2048, 256], P('loc', 'chan'), may hold values 0 or 1
- group_map: int32 [256], replicated, may hold values from 0 to 63, as said below
- embed_weight: bfloat16 [256, 2048], P(None, 'loc'), may hold values from -0.375 to 0.375
- mask_token: bfloat16 [2048], replicated, may hold values from -6 to 6
- chan_embed: bfloat16 [256, 2048], P('chan'), may hold values from -3 to 3
- agg_weight: float32 [256], P('chan'), may hold values from 0.5 to 2
- query_key: bfloat16 [16, 2048], replicated, may hold values from -0.02734375 to 0.02734375
- group_bias: float32 [16, 64], replicated, may hold values from -0.5 to 255
- norm_gain: float32 [2048], replicated, may hold values from 0.25 to 1.75
- head_weight: bfloat16 [2048, 256, 256], P(None, 'chan'), may hold values from -0.125 to 0.125
- head_bias: float32 [256, 256], P('chan'), may hold values from -3 to 3
Outputs:
- rebuilt: bfloat16 [2048, 256, 256], P('loc', 'chan')
The draws below stay inside these ranges and needn't reach their ends.
Inputs may be any that keep to these rules, and one draw needn't show every extreme that they name: `group_map`: the 4 channels of each bundle (channels k * 4 to k * 4 + 3) name at most two distinct groups.
All inputs are finite; a program needn't handle non-finite values. No bound on the sum of `patch_mask` on one device may be relied on, other than what follows from the above.
Results may differ from the reference program's by a relative error of at most 0.0051.
Values may be sent and summed in bfloat16 or wider, within the bound.
A program may use at most 64 MiB of HBM per device.

```python
import math
import jax
import jax.numpy as jnp
from jax import lax

C = 256
E = 2048
P_SIZE = 256
G = 64
H = 16
BUNDLE = 4
LOCS = 2048


def draw_group_map(key, part):
    bundles = C // BUNDLE
    key_first, key_shift, key_pick = jax.random.split(jax.random.fold_in(key, 11), 3)
    first_group = jax.random.randint(key_first, (bundles,), 0, G)
    second_group = (first_group + jax.random.randint(key_shift, (bundles,), 1, G)) % G
    picked = jax.random.randint(key_pick, (bundles, BUNDLE), 0, 2)
    leading = jnp.arange(BUNDLE)[None, :] == 0
    picked = jnp.where(leading, 0, picked)
    groups = jnp.where(picked == 1, second_group[:, None], first_group[:, None])
    return groups.reshape(C).astype(jnp.int32)


def draw_group_bias(key, part):
    key_base, key_top, key_amount = jax.random.split(jax.random.fold_in(key, 23), 3)
    baseline = jax.random.uniform(key_base, (H, G), jnp.float32, -0.5, 0.5)
    top_group = jax.random.randint(key_top, (H,), 0, G)
    amount = jax.random.uniform(key_amount, (H,), jnp.float32, 2.0, 4.0)
    group_ids = jnp.arange(G)[None, :]
    on_top = group_ids == top_group[:, None]
    biased = baseline + jnp.where(on_top, amount[:, None], 0.0)
    return biased.astype(jnp.float32)


def touch_ends(values, stream_key, least, high):
    shape = values.shape
    index_at = [jax.random.randint(jax.random.fold_in(stream_key, axis), (), 0, shape[axis]) for axis in range(len(shape))]
    values = values.at[tuple(index_at)].set(least)
    longest = shape.index(max(shape))
    index_at[longest] = (index_at[longest] + 1) % shape[longest]
    return values.at[tuple(index_at)].set(high)


def block_levels(stream_key, shape, cuts, least, largest):
    gain, own = 1.0, jax.random.fold_in(stream_key, 6)
    for position, blocks in cuts:
        steps = jnp.exp(jax.random.uniform(jax.random.fold_in(own, position), (blocks,), jnp.float32, least / len(cuts), largest / len(cuts)))
        gain = gain * jnp.repeat(steps, shape[position] // blocks).reshape([-1 if axis == position else 1 for axis in range(len(shape))])
    return gain


def normal_values(stream_key, extent, width, bound, cuts=(), kind=jnp.bfloat16):
    array = jax.random.normal(stream_key, extent, jnp.float32) * width
    if len(cuts) > 0:
        array = block_levels(stream_key, extent, cuts, -0.22, 0.18) * array
    return jnp.clip(array, min=-bound, max=bound).astype(kind)


def setup_inputs(seed: int = 0) -> dict:
    key_list = jax.random.split(jax.random.key(seed), 13)
    pixels = normal_values(key_list[0], (LOCS, C, P_SIZE), 1.0, 6.0, ((0, 8), (1, 64)))
    patch_mask = touch_ends((jax.random.randint(key_list[1], (LOCS, C), 0, 4) < 3).astype(jnp.int32), jax.random.fold_in(key_list[1], 1), 0, 1)
    group_map = draw_group_map(jax.random.fold_in(key_list[12], 71), 0)
    embed_weight = normal_values(key_list[3], (P_SIZE, E), P_SIZE ** -0.5, 0.375, ((1, 8),))
    mask_token = normal_values(key_list[4], (E,), 1.0, 6.0)
    chan_embed = normal_values(key_list[5], (C, E), 0.5, 3.0, ((0, 64),))
    agg_weight = jnp.clip(jnp.exp(math.log(2.0) - 1.3862944 * jax.random.uniform(key_list[6], (C,), jnp.float32) ** block_levels(key_list[6], (C,), ((0, 64),), -0.2, 0.2)), 0.5, 2.0)
    query_key = normal_values(key_list[7], (H, E), (25 * E) ** -0.5, 0.02734375)
    group_bias = draw_group_bias(jax.random.fold_in(key_list[12], 71), 0)
    norm_gain = jnp.clip(1.0 + 0.15 * jax.random.normal(key_list[9], (E,), jnp.float32), 0.25, 1.75)
    head_weight = normal_values(key_list[10], (E, C, P_SIZE), E ** -0.5, 0.125, ((1, 64),))
    head_bias = normal_values(key_list[11], (C, P_SIZE), 0.5, 3.0, ((0, 64),), jnp.float32)
    return {"pixels": pixels, "patch_mask": patch_mask, "group_map": group_map, "embed_weight": embed_weight, "mask_token": mask_token, "chan_embed": chan_embed, "agg_weight": agg_weight, "query_key": query_key, "group_bias": group_bias, "norm_gain": norm_gain, "head_weight": head_weight, "head_bias": head_bias}


def slot_tables(group_map):
    bundled = group_map.reshape(C // BUNDLE, BUNDLE)
    lowest = lax.optimization_barrier(jnp.min(bundled, axis=1))
    highest = lax.optimization_barrier(jnp.max(bundled, axis=1))
    slot_index = (bundled != lowest[:, None]).astype(jnp.int32)
    choose = slot_index[:, None, :] == jnp.arange(2, dtype=jnp.int32)[None, :, None]
    slot_group = jnp.stack([lowest, highest], axis=1).reshape(C // 2)
    to_group = jnp.arange(G, dtype=jnp.int32)[:, None] == slot_group[None, :]
    return (choose, to_group)

def attend(aggregate, query_key, group_bias, norm_gain):
    row_count = aggregate.shape[0]
    scores = jnp.einsum('lge,he->lhg', aggregate, query_key.astype(jnp.float32), precision=lax.Precision.HIGHEST) + group_bias[None]
    weights = jax.nn.softmax(scores, axis=-1)
    pooled = jnp.einsum('lhg,lghd->lhd', weights, aggregate.reshape(row_count, G, H, E // H), precision=lax.Precision.HIGHEST).reshape(row_count, E)
    inverse_rms = lax.rsqrt(lax.optimization_barrier(jnp.mean(pooled * pooled, axis=-1, keepdims=True)) + 1e-06)
    return (pooled * inverse_rms * norm_gain[None]).astype(jnp.bfloat16)

def reference(pixels, patch_mask, group_map, embed_weight, mask_token, chan_embed, agg_weight, query_key, group_bias, norm_gain, head_weight, head_bias):
    choose, to_group = slot_tables(group_map)
    flat_heads = head_weight.reshape(E, C * P_SIZE)
    flat_bias = head_bias.reshape(1, C * P_SIZE).astype(jnp.float32)
    block_rows = 64

    def location_block(inputs):
        block_pixels, block_mask = inputs
        projected = jnp.dot(block_pixels.reshape(block_rows * C, P_SIZE), embed_weight, preferred_element_type=jnp.float32).reshape(block_rows, C, E)
        pre_act = jnp.where(block_mask[:, :, None] == 1, mask_token.astype(jnp.float32)[None, None, :], projected) + chan_embed.astype(jnp.float32)[None]
        weighted = (jax.nn.gelu(pre_act, approximate=False) * agg_weight[None, :, None]).astype(jnp.bfloat16)
        bundle_sums = jnp.einsum('lbke,bsk->lbse', weighted.reshape(block_rows, C // BUNDLE, BUNDLE, E).astype(jnp.float32), choose.astype(jnp.float32), precision=lax.Precision.HIGHEST)
        bundle_sums = bundle_sums.reshape(block_rows, C // 2, E).astype(jnp.bfloat16)
        aggregate = jnp.einsum('gq,lqe->lge', to_group.astype(jnp.float32), bundle_sums.astype(jnp.float32), precision=lax.Precision.HIGHEST)
        joined_tokens = attend(aggregate, query_key, group_bias, norm_gain)
        decoded = jnp.dot(joined_tokens, flat_heads, preferred_element_type=jnp.float32) + flat_bias
        return decoded.astype(jnp.bfloat16).reshape(block_rows, C, P_SIZE)
    blocks = LOCS // block_rows
    rebuilt = lax.map(location_block, (pixels.reshape(blocks, block_rows, C, P_SIZE), patch_mask.reshape(blocks, block_rows, C)))
    return rebuilt.reshape(LOCS, C, P_SIZE)
```

```python
import math

import jax
import jax.numpy as jnp
from jax import lax
from jax.sharding import PartitionSpec as P

C = 256
E = 2048
G = 64
H = 16
BUNDLE = 4


def shards(
    pixels,
    patch_mask,
    group_map,
    embed_weight,
    mask_token,
    chan_embed,
    agg_weight,
    query_key,
    group_bias,
    norm_gain,
    head_weight,
    head_bias,
):
    locs, own_channels, pixel_count = pixels.shape
    peers = lax.axis_size("chan")
    bundled = group_map.reshape(C // BUNDLE, BUNDLE)
    lowest = jnp.min(bundled, axis=1)
    highest = jnp.max(bundled, axis=1)
    slot_group = jnp.stack([lowest, highest], axis=1)
    me = lax.axis_index("chan")
    own = lax.dynamic_slice_in_dim(bundled, me, 1, 0)[0]
    own_slot = (own != jnp.min(own)).astype(jnp.int32)
    choose = own_slot[None, :] == jnp.arange(2)[:, None]

    loc_peers = lax.axis_size("loc")
    copies = lax.all_to_all(
        jnp.broadcast_to(embed_weight[None], (loc_peers, *embed_weight.shape)), "loc", 0, 0, tiled=True
    )
    weight = jnp.moveaxis(copies, 0, 1).reshape(pixel_count, E)
    projected = jnp.dot(
        pixels.reshape(locs * own_channels, pixel_count), weight, preferred_element_type=jnp.float32
    ).reshape(locs, own_channels, E)
    hidden = (patch_mask == 1)[:, :, None]
    pre = jnp.where(hidden, mask_token.astype(jnp.float32)[None, None], projected)
    pre = pre + chan_embed.astype(jnp.float32)[None]
    weighted = pre * (1.0 + lax.erf(pre * (1.0 / math.sqrt(2.0)))) * (0.5 * agg_weight)[None, :, None]
    weighted = weighted.astype(jnp.bfloat16)
    sums = jnp.einsum(
        "lke,sk->sle", weighted, choose.astype(jnp.bfloat16), preferred_element_type=jnp.float32
    ).astype(jnp.bfloat16)
    part = jnp.einsum("sle,he->slh", sums, query_key, preferred_element_type=jnp.float32)
    part = part.reshape(2, locs * H)
    every = lax.all_gather(part, "chan", axis=0, tiled=True)
    to_group = (jnp.arange(G)[:, None] == slot_group.reshape(-1)[None]).astype(jnp.float32)
    scores = jnp.dot(to_group, every, precision=lax.Precision.HIGHEST).reshape(G, locs, H)
    scores = scores + group_bias.T[:, None, :]
    attn = jax.nn.softmax(scores, axis=0)
    own_group = jnp.stack([jnp.min(own), jnp.max(own)])
    own_attn = jnp.take(attn, own_group, axis=0)
    pooled = (sums.reshape(2, locs, H, E // H) * own_attn[..., None]).sum(0).reshape(locs, E)
    pooled = lax.psum_scatter(pooled, "chan", scatter_dimension=0, tiled=True)
    inverse = lax.rsqrt(jnp.mean(pooled * pooled, axis=-1, keepdims=True) + 1e-06)
    joined = (pooled * inverse * norm_gain[None]).astype(jnp.bfloat16)
    joined = lax.all_gather(joined, "chan", axis=0, tiled=True)
    decoded = jnp.dot(
        joined, head_weight.reshape(E, own_channels * pixel_count), preferred_element_type=jnp.float32
    )
    decoded = decoded + head_bias.reshape(1, own_channels * pixel_count)
    return decoded.astype(jnp.bfloat16).reshape(locs, own_channels, pixel_count)


def solution(mesh):
    return jax.shard_map(
        shards,
        mesh=mesh,
        in_specs=(
            P("loc", "chan", None),
            P("loc", "chan"),
            P(),
            P(None, "loc"),
            P(),
            P("chan", None),
            P("chan"),
            P(),
            P(),
            P(),
            P(None, "chan", None),
            P("chan", None),
        ),
        out_specs=P("loc", "chan", None),
        check_vma=False,
    )
```

```python
import functools
import math

import jax
import jax.numpy as jnp
from jax import lax
from jax.experimental import pallas as pl
from jax.experimental.pallas import tpu as pltpu
from jax.sharding import PartitionSpec as P

C = 256
E = 2048
G = 64
H = 16
BUNDLE = 4
LOCS = 256
CHAN = 64
ZS = 16
BLOCK = 256
BF = jnp.bfloat16
F32 = jnp.float32
MESH = pl.DeviceIdType.MESH


def split(value, parts):
    pieces = []
    for _ in range(parts - 1):
        piece = value.astype(BF)
        pieces.append(piece)
        value = value - piece.astype(F32)
    return [*pieces, value.astype(BF)]


def exact_dot(onehot, value):
    return sum(jnp.dot(onehot, piece, preferred_element_type=F32) for piece in split(value, 3))


def kernel(
    px,
    aux,
    emb,
    token,
    ce,
    agg,
    gm_s,
    gm_v,
    qk,
    bias,
    gain,
    out,
    wg,
    b,
    pre,
    acc,
    expand,
    sbuf,
    rbuf,
    obuf,
    abuf,
    lhs,
    ps,
    pr,
    own,
    ys,
    yr,
    zs,
    zr,
    zf,
    ssb,
    ssr,
    jt,
    esem,
    rsem,
    psem,
    ssem,
    srsem,
    csem,
    crsem,
    yrsem,
    zrsem,
    qrsem,
    jsem,
    jz,
    jy,
    jc,
    jd,
):
    ci = lax.axis_index("chan")
    li = lax.axis_index("loc")
    core = ci % 2
    z = (ci // 2) % ZS
    ylo = ci // (2 * ZS)
    x = li % 4
    yhi = li // 4
    way = 1 - 2 * core
    partner = ci + way
    ypartner = (ci + 2 * ZS) % CHAN
    nxt = yhi * 4 + (x + way + 4) % 4
    prv = yhi * 4 + (x - way + 4) % 4
    cross_loc = (1 - yhi) * 4 + x

    def at(chan, loc=None):
        return {"chan": chan, "loc": li if loc is None else loc}

    def rdma(src, dst, send, recv, where):
        return pltpu.make_async_remote_copy(
            src_ref=src, dst_ref=dst, send_sem=send, recv_sem=recv, device_id=where, device_id_type=MESH
        )

    def await_bytes(ref, sem):
        pltpu.make_async_copy(ref, ref, sem).wait()

    barrier = pltpu.get_barrier_semaphore()
    pl.semaphore_signal(barrier, inc=1, device_id=at(ci, nxt), device_id_type=MESH)
    pl.semaphore_signal(barrier, inc=1, device_id=at(ci, prv), device_id_type=MESH)
    pl.semaphore_signal(barrier, inc=1, device_id=at(ypartner, cross_loc), device_id_type=MESH)

    @pl.loop(1, CHAN)
    def _(d):
        pl.semaphore_signal(barrier, inc=1, device_id=at((ci + d) % CHAN), device_id_type=MESH)

    def place(t, row):
        return ((yhi + row) % 2) * 4 + (x + way * ((3 * t * t - 5 * t) // 2) + 8) % 4

    swapped = {1: 1, 2: 4, 3: 5, 4: 2, 5: 3, 6: 6, 7: 7}

    def half(step):
        return wg.at[place(step // 2, step % 2), core]

    def pass_on(step, to, loc):
        rdma(half(step), half(step), esem.at[0], rsem.at[to], at(ci, loc)).start()

    def to_partner(step):
        rdma(half(step), half(step), esem.at[0], psem.at[swapped[step]], at(partner)).start()

    def arrived(step):
        await_bytes(half(step), rsem.at[step])

    base = ci * BUNDLE
    groups = [gm_s[base + k] for k in range(BUNDLE)]
    low = jnp.minimum(jnp.minimum(groups[0], groups[1]), jnp.minimum(groups[2], groups[3]))
    weights = []
    for k in range(BUNDLE):
        full = 0.5 * agg[k]
        second = jnp.where(groups[k] != low, full, 0.0)
        weights.append((full - second, second))

    wg[li] = emb[...].reshape(2, 128, BLOCK)
    acc[...] = jnp.zeros_like(acc)
    zr[z] = jnp.zeros((8, 1024), BF)
    row16 = lax.broadcasted_iota(jnp.int32, (128, BLOCK), 0)

    @pl.loop(0, 8)
    def _(step):
        @pl.when(step == 1)
        def _():
            pl.semaphore_wait(barrier, CHAN - 1 + 3)
            mine = emb.at[pl.ds(pl.multiple_of(core * 128, 128), 128), :]
            dst = wg.at[li, core]
            rdma(mine, dst, esem.at[0], rsem.at[1], at(ypartner, cross_loc)).start()
            rdma(mine, dst, esem.at[0], rsem.at[2], at(ci, nxt)).start()
            rdma(mine, dst, esem.at[0], rsem.at[4], at(ci, prv)).start()
            arrived(1)
            pass_on(1, 3, nxt)
            pass_on(1, 5, prv)
            to_partner(1)
            arrived(2)
            pass_on(2, 6, nxt)
            to_partner(2)
            arrived(4)
            to_partner(4)

        @pl.when(step == 3)
        def _():
            arrived(3)
            pass_on(3, 7, nxt)
            to_partner(3)
            arrived(5)
            to_partner(5)

        @pl.when(step == 5)
        def _():
            arrived(6)
            to_partner(6)

        @pl.when(step == 6)
        def _():
            arrived(7)
            to_partner(7)

        t, row = step // 2, step % 2
        j = place(t, row)

        @pl.when(step > 0)
        def _():
            await_bytes(wg.at[j, 1 - core], psem.at[step])

        columns = pl.ds(pl.multiple_of(j * BLOCK, BLOCK), BLOCK)
        weight = wg[j].reshape(BLOCK, BLOCK)
        extra = jnp.where(row16 == 0, token[:, columns].astype(F32), 0.0)
        embeds = ce[:, columns].astype(F32)
        for k in range(BUNDLE):
            extra = jnp.where(row16 == 1 + k, embeds[k : k + 1], extra)
        extra = extra.astype(BF)

        @pl.loop(0, BUNDLE)
        def _(k):
            rows = pl.ds(pl.multiple_of(k * LOCS, LOCS), LOCS)
            pre[rows, :] = jnp.dot(px[rows, :], weight, preferred_element_type=F32) + jnp.dot(
                aux[rows, :], extra, preferred_element_type=F32
            )

        @pl.loop(0, LOCS // 32)
        def _(chunk):
            first, second = None, None
            for k in range(BUNDLE):
                v = pre[pl.ds(pl.multiple_of(k * LOCS + chunk * 32, 32), 32), :]
                g = v + v * lax.erf(v * (1.0 / math.sqrt(2.0)))
                w0, w1 = weights[k]
                first = g * w0 if first is None else first + g * w0
                second = g * w1 if second is None else second + g * w1
            b[j, pl.ds(pl.multiple_of(chunk * 32, 32), 32), :] = first.astype(BF)
            b[j, pl.ds(pl.multiple_of(LOCS + chunk * 32, 32), 32), :] = second.astype(BF)

        q = jnp.concatenate([qk[:, columns]] * 8, axis=0)
        acc[...] += lax.dot_general(b[j], q, (((1,), (1,)), ((), ())), preferred_element_type=F32)
        p = lax.broadcasted_iota(jnp.int32, (BLOCK, BLOCK), 0) % H
        head = 2 * step + lax.broadcasted_iota(jnp.int32, (BLOCK, BLOCK), 1) // 128
        expand[step] = jnp.where(p == head, 1.0, 0.0).astype(BF)

    lane = lax.broadcasted_iota(jnp.int32, (CHAN, 128), 1)
    part = jnp.zeros((CHAN, 128), F32)
    for q in range(8):
        part = part + jnp.where(lane // H == q, acc[q * 64 : (q + 1) * 64, :], 0.0)
    sbuf[...] = part.reshape(CHAN, 1, 128)

    @pl.loop(1, CHAN)
    def _(d):
        peer = (ci + d) % CHAN
        rdma(sbuf.at[peer], rbuf.at[ci], ssem.at[0], srsem.at[0], at(peer)).start()

    rbuf[ci] = sbuf[ci]
    gmap = jnp.broadcast_to(gm_v[...].astype(F32), (8, C))
    wide = lax.broadcasted_iota(jnp.int32, (CHAN, C), 1)
    bund = lax.broadcasted_iota(jnp.int32, (CHAN, C), 0)
    inside = wide // BUNDLE == bund
    lows = jnp.min(jnp.where(inside, gmap[0:1], 1e9), axis=1, keepdims=True)
    highs = jnp.max(jnp.where(inside, gmap[0:1], -1.0), axis=1, keepdims=True)
    gcol = lax.broadcasted_iota(jnp.int32, (CHAN, G), 1).astype(F32)
    from_group = [jnp.where(v == gcol, 1.0, 0.0).astype(BF) for v in (lows, highs)]
    to_group = [f.astype(F32).T.astype(BF) for f in from_group]

    await_bytes(rbuf.at[pl.ds(0, CHAN - 1)], srsem.at[0])
    got = rbuf[...].reshape(CHAN, 128)
    mixed = jnp.where(lane < 64, exact_dot(to_group[0], got), exact_dot(to_group[1], got))
    scores = mixed + pltpu.roll(mixed, 64, 1) + bias[...]
    top = jnp.max(scores, axis=0, keepdims=True)
    raised = jnp.exp(scores - top)
    attn = raised / jnp.sum(raised, axis=0, keepdims=True)
    back = jnp.where(lane < 64, exact_dot(from_group[0], attn), exact_dot(from_group[1], attn))
    obuf[...] = back.reshape(CHAN, 1, 128)

    @pl.loop(1, CHAN)
    def _(d):
        peer = (ci + d) % CHAN
        rdma(obuf.at[peer], abuf.at[ci], ssem.at[1], srsem.at[1], at(peer)).start()

    abuf[ci] = obuf[ci]
    await_bytes(abuf.at[pl.ds(0, CHAN - 1)], srsem.at[1])
    high, rest = split(abuf[...].reshape(CHAN, 128), 2)
    high, rest = high.astype(F32), rest.astype(F32)
    for q in range(8):
        lhs[q * 64 : (q + 1) * 64, 0:128] = jnp.where(lane // H == q, high, 0.0).astype(BF)
        lhs[q * 64 : (q + 1) * 64, 128:256] = jnp.where(lane // H == q, rest, 0.0).astype(BF)

    def weigh(j):
        spread = jnp.dot(lhs[...], expand[j], preferred_element_type=F32)
        return spread[:LOCS] * b[j, 0:LOCS, :].astype(F32) + spread[LOCS:] * b[j, LOCS:, :].astype(F32)

    @pl.loop(0, 4)
    def _(t):
        ps[t] = weigh((1 - core) * 4 + t).astype(BF)
        rdma(ps.at[t], pr.at[t], csem.at[0], crsem.at[t], at(partner)).start()

    @pl.loop(0, 4)
    def _(t):
        own[t] = weigh(core * 4 + t)

    @pl.loop(0, 4)
    def _(t):
        await_bytes(pr.at[t], crsem.at[t])
        theirs = pl.ds(pl.multiple_of((1 - ylo) * 128, 128), 128)
        ys[t] = (own[t, theirs, :] + pr[t, theirs, :].astype(F32)).astype(BF)
        rdma(ys.at[t], yr.at[t], csem.at[1], yrsem.at[t], at(ypartner)).start()

    for t in range(4):
        mine = pl.ds(pl.multiple_of(ylo * 128, 128), 128)
        await_bytes(yr.at[t], yrsem.at[t])
        total = own[t, mine, :] + pr[t, mine, :].astype(F32) + yr[t].astype(F32)
        total = total.reshape(ZS, 8, BLOCK)
        zf[:, :, t * BLOCK : (t + 1) * BLOCK] = total
        zs[:, :, t * BLOCK : (t + 1) * BLOCK] = total.astype(BF)

    @pl.loop(1, ZS)
    def _(e):
        d = (e % 2) * ((e + 1) // 2) + (1 - e % 2) * (ZS - e // 2)
        to = (z + d) % ZS
        peer = ylo * 2 * ZS + to * 2 + core
        rdma(zs.at[to], zr.at[z], csem.at[2], zrsem.at[0], at(peer)).start()

    await_bytes(zr.at[pl.ds(0, ZS - 1)], zrsem.at[0])
    pooled = zf[z]
    for k in range(ZS):
        pooled = pooled + zr[k].astype(F32)
    squares = jnp.sum(pooled * pooled, axis=1, keepdims=True)
    ssb[...] = jnp.broadcast_to(squares, (8, 128))
    share = rdma(ssb, ssr, csem.at[3], qrsem.at[0], at(partner))
    share.start()
    scaled = pooled * gain[:, pl.ds(pl.multiple_of(core * 1024, 1024), 1024)]
    share.wait_recv()
    inverse = lax.rsqrt((squares + ssr[:, 0:1]) * (1.0 / E) + 1e-06)
    jt[core, ylo, z] = (scaled * inverse).astype(BF)

    @pl.loop(1, ZS)
    def _(e):
        d = (e % 2) * ((e + 1) // 2) + (1 - e % 2) * (ZS - e // 2)
        peer = ylo * 2 * ZS + ((z + d) % ZS) * 2 + core
        block = jt.at[core, ylo, z]
        rdma(block, block, jsem.at[0], jz.at[d], at(peer)).start()

    @pl.loop(0, ZS)
    def _(e):
        d = ((e % 2) * ((e + 1) // 2) + (1 - e % 2) * (ZS - e // 2)) % ZS
        block = jt.at[core, ylo, (z + ZS - d) % ZS]

        @pl.when(e > 0)
        def _():
            await_bytes(block, jz.at[d])

        rdma(block, block, jsem.at[1], jy.at[d], at(ypartner)).start()
        rdma(block, block, jsem.at[2], jc.at[d], at(partner)).start()

    @pl.loop(0, ZS)
    def _(e):
        d = ((e % 2) * ((e + 1) // 2) + (1 - e % 2) * (ZS - e // 2)) % ZS
        block = jt.at[core, 1 - ylo, (z + ZS - d) % ZS]
        await_bytes(block, jy.at[d])
        rdma(block, block, jsem.at[2], jd.at[d], at(partner)).start()

    @pl.loop(0, ZS)
    def _(d):
        block = (z + ZS - d) % ZS
        await_bytes(jt.at[1 - core, ylo, block], jc.at[d])
        await_bytes(jt.at[1 - core, 1 - ylo, block], jd.at[d])

    for c in range(2):
        out[:, c * 1024 : (c + 1) * 1024] = jt[c].reshape(LOCS, 1024)

    await_bytes(wg.at[pl.ds(0, 7)], esem.at[0])
    await_bytes(sbuf.at[pl.ds(0, CHAN - 1)], ssem.at[0])
    await_bytes(obuf.at[pl.ds(0, CHAN - 1)], ssem.at[1])
    await_bytes(ps, csem.at[0])
    await_bytes(ys, csem.at[1])
    await_bytes(zs.at[pl.ds(0, ZS - 1)], csem.at[2])
    share.wait_send()
    await_bytes(jt.at[0, 0, pl.ds(0, ZS - 1)], jsem.at[0])
    await_bytes(jt.at[0, 0], jsem.at[1])
    await_bytes(jt.at[0], jsem.at[2])


def shards(
    pixels,
    patch_mask,
    group_map,
    embed_weight,
    mask_token,
    chan_embed,
    agg_weight,
    query_key,
    group_bias,
    norm_gain,
    head_weight,
    head_bias,
):
    locs, own_channels, pixel_count = pixels.shape
    hidden = (patch_mask == 1).T[:, :, None]
    px = jnp.where(hidden, jnp.zeros((), BF), jnp.swapaxes(pixels, 0, 1))
    at_lane = lax.broadcasted_iota(jnp.int32, (own_channels, locs, 128), 2)
    channel = lax.broadcasted_iota(jnp.int32, (own_channels, locs, 128), 0)
    aux = ((at_lane == channel + 1) | ((at_lane == 0) & hidden)).astype(BF)
    bias = jnp.tile(group_bias.T, (1, 8))
    vmem = pl.BlockSpec(memory_space=pltpu.VMEM)
    smem = pl.BlockSpec(memory_space=pltpu.SMEM)
    dma = pltpu.SemaphoreType.DMA
    joined = pl.pallas_call(
        kernel,
        out_shape=jax.ShapeDtypeStruct((LOCS, E), BF),
        in_specs=[vmem] * 5 + [smem] * 2 + [vmem] * 4,
        out_specs=vmem,
        scratch_shapes=[
            pltpu.VMEM((8, 2, 128, BLOCK), BF),
            pltpu.VMEM((8, 2 * LOCS, BLOCK), BF),
            pltpu.VMEM((BUNDLE * LOCS, BLOCK), F32),
            pltpu.VMEM((2 * LOCS, 128), F32),
            pltpu.VMEM((8, BLOCK, BLOCK), BF),
            pltpu.VMEM((CHAN, 1, 128), F32),
            pltpu.VMEM((CHAN, 1, 128), F32),
            pltpu.VMEM((CHAN, 1, 128), F32),
            pltpu.VMEM((CHAN, 1, 128), F32),
            pltpu.VMEM((2 * LOCS, 256), BF),
            pltpu.VMEM((4, LOCS, BLOCK), BF),
            pltpu.VMEM((4, LOCS, BLOCK), BF),
            pltpu.VMEM((4, LOCS, BLOCK), F32),
            pltpu.VMEM((4, 128, BLOCK), BF),
            pltpu.VMEM((4, 128, BLOCK), BF),
            pltpu.VMEM((ZS, 8, 1024), BF),
            pltpu.VMEM((ZS, 8, 1024), BF),
            pltpu.VMEM((ZS, 8, 1024), F32),
            pltpu.VMEM((8, 128), F32),
            pltpu.VMEM((8, 128), F32),
            pltpu.VMEM((2, 2, ZS, 8, 1024), BF),
            dma((1,)),
            dma((8,)),
            dma((8,)),
            dma((2,)),
            dma((2,)),
            dma((4,)),
            dma((4,)),
            dma((4,)),
            dma((1,)),
            dma((1,)),
            dma((3,)),
            dma((ZS,)),
            dma((ZS,)),
            dma((ZS,)),
            dma((ZS,)),
        ],
        compiler_params=pltpu.CompilerParams(
            collective_id=0, has_side_effects=True, vmem_limit_bytes=32 * 1024 * 1024
        ),
    )(
        px.reshape(own_channels * locs, pixel_count),
        aux.reshape(own_channels * locs, 128),
        embed_weight,
        mask_token.reshape(1, E),
        chan_embed,
        agg_weight,
        group_map,
        group_map.reshape(1, C),
        query_key,
        bias,
        norm_gain.reshape(1, E),
    )
    decoded = jnp.dot(
        joined, head_weight.reshape(E, own_channels * pixel_count), preferred_element_type=F32
    )
    decoded = decoded + head_bias.reshape(1, own_channels * pixel_count)
    return decoded.astype(BF).reshape(locs, own_channels, pixel_count)


def solution(mesh):
    return jax.shard_map(
        shards,
        mesh=mesh,
        in_specs=(
            P("loc", "chan", None),
            P("loc", "chan"),
            P(),
            P(None, "loc"),
            P(),
            P("chan", None),
            P("chan"),
            P(),
            P(),
            P(),
            P(None, "chan", None),
            P("chan", None),
        ),
        out_specs=P("loc", "chan", None),
        check_vma=False,
    )
```

```python
import functools
import math

import jax
import jax.numpy as jnp
from jax import lax
from jax.experimental import pallas as pl
from jax.experimental.pallas import tpu as pltpu
from jax.sharding import PartitionSpec as P

C = 256
E = 2048
G = 64
H = 16
BUNDLE = 4
LOCS = 256
CHAN = 64
ZS = 16
BLOCK = 256
BF = jnp.bfloat16
F32 = jnp.float32
MESH = pl.DeviceIdType.MESH


def split(value, parts):
    pieces = []
    for _ in range(parts - 1):
        piece = value.astype(BF)
        pieces.append(piece)
        value = value - piece.astype(F32)
    return [*pieces, value.astype(BF)]


def exact_dot(onehot, value):
    return sum(jnp.dot(onehot, piece, preferred_element_type=F32) for piece in split(value, 3))


def kernel(
    pixels_h,
    mask_h,
    emb_h,
    token_h,
    ce_h,
    agg_h,
    map_h,
    gmv_h,
    qk_h,
    gbias_h,
    gain_h,
    head_h,
    hbias_h,
    out,
    raw,
    maskv,
    token,
    ce,
    agg,
    gm_s,
    gm_v,
    qk,
    gbias,
    gain,
    hraw,
    hbias,
    tokf,
    keep,
    px,
    aux,
    wd,
    dec,
    wg,
    b,
    pre,
    acc,
    expand,
    sbuf,
    rbuf,
    obuf,
    abuf,
    lhs,
    ps,
    pr,
    own,
    ys,
    yr,
    zs,
    zf,
    zr,
    rin,
    rout,
    pooled,
    ssb,
    ssr,
    jt,
    lsem,
    esem,
    rsem,
    psem,
    ssem,
    srsem,
    csem,
    crsem,
    yrsem,
    zsem,
    rinsem,
    zrsem,
    qrsem,
    jsem,
    jz,
    jy,
    jc,
    jd,
):
    ci = lax.axis_index("chan")
    li = lax.axis_index("loc")
    core = ci % 2
    z = (ci // 2) % ZS
    ylo = ci // (2 * ZS)
    x = li % 4
    yhi = li // 4
    way = 1 - 2 * core
    partner = ci + way
    ypartner = (ci + 2 * ZS) % CHAN
    nxt = yhi * 4 + (x + way + 4) % 4
    prv = yhi * 4 + (x - way + 4) % 4
    cross_loc = (1 - yhi) * 4 + x

    def at(chan, loc=None):
        return {"chan": chan, "loc": li if loc is None else loc}

    def rdma(src, dst, send, recv, where):
        return pltpu.make_async_remote_copy(
            src_ref=src, dst_ref=dst, send_sem=send, recv_sem=recv, device_id=where, device_id_type=MESH
        )

    def await_bytes(ref, sem):
        pltpu.make_async_copy(ref, ref, sem).wait()

    barrier = pltpu.get_barrier_semaphore()
    pl.semaphore_signal(barrier, inc=1, device_id=at(ci, nxt), device_id_type=MESH)
    pl.semaphore_signal(barrier, inc=1, device_id=at(ci, prv), device_id_type=MESH)
    pl.semaphore_signal(barrier, inc=1, device_id=at(ypartner, cross_loc), device_id_type=MESH)

    @pl.loop(1, CHAN)
    def _(d):
        pl.semaphore_signal(barrier, inc=1, device_id=at((ci + d) % CHAN), device_id_type=MESH)

    def load(k, src, dst):
        copy = pltpu.make_async_copy(src, dst, lsem.at[k])
        copy.start()
        return copy

    first_half = load(0, emb_h.at[pl.ds(0, 128)], wg.at[li, 0])
    other_half = load(1, emb_h.at[pl.ds(128, 128)], wg.at[li, 1])
    loads = [
        load(2, pixels_h, raw),
        load(3, mask_h, maskv),
        load(4, token_h, token),
        load(5, ce_h, ce),
        load(6, agg_h, agg),
        load(7, map_h, gm_s),
        load(8, gmv_h, gm_v),
        load(9, qk_h, qk),
        load(10, gbias_h, gbias),
        load(11, gain_h, gain),
        load(12, hbias_h, hbias),
    ]
    heads = load(13, head_h, hraw)

    def place(t, row):
        return ((yhi + row) % 2) * 4 + (x + way * ((3 * t * t - 5 * t) // 2) + 8) % 4

    swapped = {1: 1, 2: 4, 3: 5, 4: 2, 5: 3, 6: 6, 7: 7}

    def half(step):
        return wg.at[place(step // 2, step % 2), core]

    def pass_on(step, to, loc):
        rdma(half(step), half(step), esem.at[0], rsem.at[to], at(ci, loc)).start()

    def to_partner(step):
        rdma(half(step), half(step), esem.at[0], psem.at[swapped[step]], at(partner)).start()

    def arrived(step):
        await_bytes(half(step), rsem.at[step])

    for copy in loads:
        copy.wait()
    first_half.wait()
    other_half.wait()

    base = ci * BUNDLE
    groups = [gm_s[base + k] for k in range(BUNDLE)]
    low = jnp.minimum(jnp.minimum(groups[0], groups[1]), jnp.minimum(groups[2], groups[3]))
    weights = []
    for k in range(BUNDLE):
        full = 0.5 * agg[k]
        second = jnp.where(groups[k] != low, full, 0.0)
        weights.append((full - second, second))

    acc[...] = jnp.zeros_like(acc)
    tokf[...] = token[...].astype(F32)

    @pl.loop(0, BUNDLE)
    def _(c):
        hid = jnp.broadcast_to(maskv[pl.ds(c, 1), :].astype(F32), (128, LOCS)).T
        rows = pl.ds(pl.multiple_of(c * LOCS, LOCS), LOCS)
        at_lane = lax.broadcasted_iota(jnp.int32, (LOCS, 128), 1)
        aux[rows, :] = jnp.where(at_lane == 0, hid, jnp.where(at_lane == 1 + c, 1.0, 0.0)).astype(BF)
        keep[c] = 1.0 - hid

    @pl.loop(0, LOCS // 32)
    def _(i):
        rows = pl.ds(pl.multiple_of(i * 32, 32), 32)
        turned = jnp.swapaxes(raw[rows], 0, 1)
        for c in range(BUNDLE):
            shown = keep[c, rows, :]
            kept = turned[c].astype(F32) * jnp.concatenate([shown, shown], axis=1)
            px[pl.ds(pl.multiple_of(c * LOCS + i * 32, 32), 32), :] = kept.astype(BF)

    @pl.loop(0, 8)
    def _(step):
        p = lax.broadcasted_iota(jnp.int32, (BLOCK, BLOCK), 0) % H
        head = 2 * step + lax.broadcasted_iota(jnp.int32, (BLOCK, BLOCK), 1) // 128
        expand[step] = jnp.where(p == head, 1.0, 0.0).astype(BF)

    row16 = lax.broadcasted_iota(jnp.int32, (128, BLOCK), 0)

    @pl.loop(0, 8)
    def _(step):
        @pl.when(step == 1)
        def _():
            pl.semaphore_wait(barrier, CHAN - 1 + 3)
            mine = wg.at[li, core]
            dst = mine
            rdma(mine, dst, esem.at[0], rsem.at[1], at(ypartner, cross_loc)).start()
            rdma(mine, dst, esem.at[0], rsem.at[2], at(ci, nxt)).start()
            rdma(mine, dst, esem.at[0], rsem.at[4], at(ci, prv)).start()
            arrived(1)
            pass_on(1, 3, nxt)
            pass_on(1, 5, prv)
            to_partner(1)
            arrived(2)
            pass_on(2, 6, nxt)
            to_partner(2)
            arrived(4)
            to_partner(4)

        @pl.when(step == 3)
        def _():
            arrived(3)
            pass_on(3, 7, nxt)
            to_partner(3)
            arrived(5)
            to_partner(5)

        @pl.when(step == 5)
        def _():
            arrived(6)
            to_partner(6)

        @pl.when(step == 6)
        def _():
            arrived(7)
            to_partner(7)

        t, row = step // 2, step % 2
        j = place(t, row)

        @pl.when(step > 0)
        def _():
            await_bytes(wg.at[j, 1 - core], psem.at[step])

        columns = pl.ds(pl.multiple_of(j * BLOCK, BLOCK), BLOCK)
        weight = wg[j].reshape(BLOCK, BLOCK)
        hide = jnp.concatenate([tokf[pl.ds(2 * j, 1), :], tokf[pl.ds(2 * j + 1, 1), :]], axis=1)
        extra = jnp.where(row16 == 0, hide, 0.0)
        embeds = ce[:, columns].astype(F32)
        for k in range(BUNDLE):
            extra = jnp.where(row16 == 1 + k, embeds[k : k + 1], extra)
        extra = extra.astype(BF)

        @pl.loop(0, BUNDLE)
        def _(k):
            rows = pl.ds(pl.multiple_of(k * LOCS, LOCS), LOCS)
            pre[rows, :] = jnp.dot(px[rows, :], weight, preferred_element_type=F32) + jnp.dot(
                aux[rows, :], extra, preferred_element_type=F32
            )

        @pl.loop(0, LOCS // 32)
        def _(chunk):
            first, second = None, None
            for k in range(BUNDLE):
                v = pre[pl.ds(pl.multiple_of(k * LOCS + chunk * 32, 32), 32), :]
                g = v + v * lax.erf(v * (1.0 / math.sqrt(2.0)))
                w0, w1 = weights[k]
                first = g * w0 if first is None else first + g * w0
                second = g * w1 if second is None else second + g * w1
            b[j, pl.ds(pl.multiple_of(chunk * 32, 32), 32), :] = first.astype(BF)
            b[j, pl.ds(pl.multiple_of(LOCS + chunk * 32, 32), 32), :] = second.astype(BF)

        q = jnp.concatenate([qk[:, columns]] * 8, axis=0)
        acc[...] += lax.dot_general(b[j], q, (((1,), (1,)), ((), ())), preferred_element_type=F32)

    lane = lax.broadcasted_iota(jnp.int32, (CHAN, 128), 1)
    part = jnp.zeros((CHAN, 128), F32)
    for q in range(8):
        part = part + jnp.where(lane // H == q, acc[q * 64 : (q + 1) * 64, :], 0.0)
    sbuf[...] = part.reshape(CHAN, 1, 128)

    @pl.loop(1, CHAN)
    def _(d):
        peer = (ci + d) % CHAN
        rdma(sbuf.at[peer], rbuf.at[ci], ssem.at[0], srsem.at[0], at(peer)).start()

    rbuf[ci] = sbuf[ci]
    gmap = jnp.broadcast_to(gm_v[...].astype(F32), (8, C))
    wide = lax.broadcasted_iota(jnp.int32, (CHAN, C), 1)
    bund = lax.broadcasted_iota(jnp.int32, (CHAN, C), 0)
    inside = wide // BUNDLE == bund
    lows = jnp.min(jnp.where(inside, gmap[0:1], 1e9), axis=1, keepdims=True)
    highs = jnp.max(jnp.where(inside, gmap[0:1], -1.0), axis=1, keepdims=True)
    gcol = lax.broadcasted_iota(jnp.int32, (CHAN, G), 1).astype(F32)
    from_group = [jnp.where(v == gcol, 1.0, 0.0).astype(BF) for v in (lows, highs)]
    to_group = [f.astype(F32).T.astype(BF) for f in from_group]

    bias = jnp.concatenate([gbias[...]] * 8, axis=0).T
    heads.wait()

    @pl.loop(0, E // 32)
    def _(i):
        rows = pl.ds(pl.multiple_of(i * 32, 32), 32)
        wd[:, rows, :] = jnp.swapaxes(hraw[rows], 0, 1)

    await_bytes(rbuf.at[pl.ds(0, CHAN - 1)], srsem.at[0])
    got = rbuf[...].reshape(CHAN, 128)
    mixed = jnp.where(lane < 64, exact_dot(to_group[0], got), exact_dot(to_group[1], got))
    scores = mixed + pltpu.roll(mixed, 64, 1) + bias
    top = jnp.max(scores, axis=0, keepdims=True)
    raised = jnp.exp(scores - top)
    attn = raised / jnp.sum(raised, axis=0, keepdims=True)
    back = jnp.where(lane < 64, exact_dot(from_group[0], attn), exact_dot(from_group[1], attn))
    obuf[...] = back.reshape(CHAN, 1, 128)

    @pl.loop(1, CHAN)
    def _(d):
        peer = (ci + d) % CHAN
        rdma(obuf.at[peer], abuf.at[ci], ssem.at[1], srsem.at[1], at(peer)).start()

    abuf[ci] = obuf[ci]
    await_bytes(abuf.at[pl.ds(0, CHAN - 1)], srsem.at[1])
    high, rest = split(abuf[...].reshape(CHAN, 128), 2)
    high, rest = high.astype(F32), rest.astype(F32)
    for q in range(8):
        lhs[q * 64 : (q + 1) * 64, 0:128] = jnp.where(lane // H == q, high, 0.0).astype(BF)
        lhs[q * 64 : (q + 1) * 64, 128:256] = jnp.where(lane // H == q, rest, 0.0).astype(BF)

    def weigh(j):
        spread = jnp.dot(lhs[...], expand[j], preferred_element_type=F32)
        return spread[:LOCS] * b[j, 0:LOCS, :].astype(F32) + spread[LOCS:] * b[j, LOCS:, :].astype(F32)

    @pl.loop(0, 4)
    def _(t):
        ps[t] = weigh((1 - core) * 4 + t).astype(BF)
        rdma(ps.at[t], pr.at[t], csem.at[0], crsem.at[t], at(partner)).start()

    @pl.loop(0, 4)
    def _(t):
        own[t] = weigh(core * 4 + t)

    @pl.loop(0, 4)
    def _(t):
        await_bytes(pr.at[t], crsem.at[t])
        theirs = pl.ds(pl.multiple_of((1 - ylo) * 128, 128), 128)
        ys[t] = (own[t, theirs, :] + pr[t, theirs, :].astype(F32)).astype(BF)
        rdma(ys.at[t], yr.at[t], csem.at[1], yrsem.at[t], at(ypartner)).start()

    def zdev(to):
        return at(ylo * 2 * ZS + to * 2 + core)

    @pl.loop(0, 4)
    def _(t):
        mine = pl.ds(pl.multiple_of(ylo * 128, 128), 128)
        await_bytes(yr.at[t], yrsem.at[t])
        total = own[t, mine, :] + pr[t, mine, :].astype(F32) + yr[t].astype(F32)
        total = total.reshape(ZS, 8, BLOCK)
        zf[t] = total
        zs[t] = total.astype(BF)
        for d in (8, 7, 6, 5):
            to, via = (z + d) % ZS, (z + d - 4) % ZS
            rdma(zs.at[t, to], rin.at[t, 0, d - 5], zsem.at[0], rinsem.at[0, t], zdev(via)).start()
            if d < 8:
                to, via = (z + ZS - d) % ZS, (z + ZS - d + 4) % ZS
                rdma(zs.at[t, to], rin.at[t, 1, d - 5], zsem.at[0], rinsem.at[1, t], zdev(via)).start()
        for d in (3, 2, 1):
            for q, to in enumerate(((z + d) % ZS, (z + ZS - d) % ZS)):
                rdma(zs.at[t, to], zr.at[t, q, d - 1], zsem.at[0], zrsem.at[t], zdev(to)).start()

    @pl.loop(0, 4)
    def _(t):
        for q, to, n in ((0, (z + 4) % ZS, 4), (1, (z + ZS - 4) % ZS, 3)):
            await_bytes(rin.at[t, q, pl.ds(0, n)], rinsem.at[q, t])
            total = zf[t, to]
            for d in range(n):
                total = total + rin[t, q, d].astype(F32)
            rout[t, q] = total.astype(BF)
            rdma(rout.at[t, q], zr.at[t, q, 3], zsem.at[1], zrsem.at[t], zdev(to)).start()

    squares = jnp.zeros((8, 1), F32)
    for t in range(4):
        await_bytes(zr.at[t], zrsem.at[t])
        total = zf[t, z]
        for q in range(2):
            for d in range(4):
                total = total + zr[t, q, d].astype(F32)
        pooled[:, t * BLOCK : (t + 1) * BLOCK] = total
        squares = squares + jnp.sum(total * total, axis=1, keepdims=True)
    ssb[...] = jnp.broadcast_to(squares, (8, 128))
    share = rdma(ssb, ssr, csem.at[3], qrsem.at[0], at(partner))
    share.start()
    scaled = pooled[...] * gain[:, pl.ds(pl.multiple_of(core * 1024, 1024), 1024)]
    share.wait_recv()
    inverse = lax.rsqrt((squares + ssr[:, 0:1]) * (1.0 / E) + 1e-06)
    jt[core, ylo, z] = (scaled * inverse).astype(BF)

    def row_block(row, d):
        return jt.at[core, row, (z + ZS - d) % ZS]

    def spread(d, way_z, steps):
        for n in steps:
            block = row_block(ylo, d)
            there = (d + way_z * n) % ZS
            rdma(block, block, jsem.at[0], jz.at[there], zdev((z + ZS + way_z * n) % ZS)).start()

    def share_block(d):
        block = row_block(ylo, d)
        rdma(block, block, jsem.at[1], jy.at[d], at(ypartner)).start()
        rdma(block, block, jsem.at[2], jc.at[d], at(partner)).start()

    for n in (4, 3, 2, 1):
        spread(0, 1, (n,))
        spread(0, -1, (n,))
    share_block(0)
    order = (4, 12, 1, 15, 2, 14, 3, 13, 5, 11, 6, 10, 7, 9, 8)
    for d in order:
        await_bytes(row_block(ylo, d), jz.at[d])
        if d == 4:
            spread(4, 1, (4, 3, 2, 1))
        if d == 12:
            spread(12, -1, (3, 2, 1))
        share_block(d)
    for d in (0, *order):
        block = row_block(1 - ylo, d)
        await_bytes(block, jy.at[d])
        rdma(block, block, jsem.at[2], jd.at[d], at(partner)).start()

    def decode(row):
        sides = [jt[c, row].reshape(128, 1024) for c in range(2)]

        @pl.loop(0, BUNDLE)
        def _(c):
            total = jnp.dot(sides[0], wd[c, 0:1024, :], preferred_element_type=F32)
            total = total + jnp.dot(sides[1], wd[c, 1024:2048, :], preferred_element_type=F32)
            dec[c] = (total + hbias[pl.ds(c, 1), :]).astype(BF)

        @pl.loop(0, 4)
        def _(i):
            rows = pl.ds(pl.multiple_of(row * 128 + i * 32, 32), 32)
            out[rows] = jnp.swapaxes(dec[:, pl.ds(pl.multiple_of(i * 32, 32), 32), :], 0, 1)

    for d in range(ZS):
        block = jt.at[1 - core, ylo, (z + ZS - d) % ZS]
        await_bytes(block, jc.at[d])
    decode(ylo)
    for d in range(ZS):
        block = jt.at[1 - core, 1 - ylo, (z + ZS - d) % ZS]
        await_bytes(block, jd.at[d])
    decode(1 - ylo)

    await_bytes(wg.at[pl.ds(0, 7)], esem.at[0])
    await_bytes(sbuf.at[pl.ds(0, CHAN - 1)], ssem.at[0])
    await_bytes(obuf.at[pl.ds(0, CHAN - 1)], ssem.at[1])
    await_bytes(ps, csem.at[0])
    await_bytes(ys, csem.at[1])
    await_bytes(zs.at[:, pl.ds(0, 13)], zsem.at[0])
    await_bytes(rout, zsem.at[1])
    share.wait_send()
    await_bytes(jt.at[0, 0, pl.ds(0, ZS - 1)], jsem.at[0])
    await_bytes(jt.at[0, 0], jsem.at[1])
    await_bytes(jt.at[0], jsem.at[2])


def shards(
    pixels,
    patch_mask,
    group_map,
    embed_weight,
    mask_token,
    chan_embed,
    agg_weight,
    query_key,
    group_bias,
    norm_gain,
    head_weight,
    head_bias,
):
    vmem = pl.BlockSpec(memory_space=pltpu.VMEM)
    hbm = pl.BlockSpec(memory_space=pltpu.HBM)
    dma = pltpu.SemaphoreType.DMA
    return pl.pallas_call(
        kernel,
        out_shape=jax.ShapeDtypeStruct(pixels.shape, BF),
        in_specs=[hbm] * 13,
        out_specs=vmem,
        scratch_shapes=[
            pltpu.VMEM((LOCS, BUNDLE, BLOCK), BF),
            pltpu.VMEM((BUNDLE, LOCS), jnp.int32),
            pltpu.VMEM((16, 128), BF),
            pltpu.VMEM((BUNDLE, E), BF),
            pltpu.SMEM((BUNDLE,), F32),
            pltpu.SMEM((C,), jnp.int32),
            pltpu.VMEM((1, C), jnp.int32),
            pltpu.VMEM((H, E), BF),
            pltpu.VMEM((H, G), F32),
            pltpu.VMEM((1, E), F32),
            pltpu.VMEM((E, BUNDLE, BLOCK), BF),
            pltpu.VMEM((BUNDLE, BLOCK), F32),
            pltpu.VMEM((16, 128), F32),
            pltpu.VMEM((BUNDLE, LOCS, 128), F32),
            pltpu.VMEM((BUNDLE * LOCS, BLOCK), BF),
            pltpu.VMEM((BUNDLE * LOCS, 128), BF),
            pltpu.VMEM((BUNDLE, E, BLOCK), BF),
            pltpu.VMEM((BUNDLE, 128, BLOCK), BF),
            pltpu.VMEM((8, 2, 128, BLOCK), BF),
            pltpu.VMEM((8, 2 * LOCS, BLOCK), BF),
            pltpu.VMEM((BUNDLE * LOCS, BLOCK), F32),
            pltpu.VMEM((2 * LOCS, 128), F32),
            pltpu.VMEM((8, BLOCK, BLOCK), BF),
            pltpu.VMEM((CHAN, 1, 128), F32),
            pltpu.VMEM((CHAN, 1, 128), F32),
            pltpu.VMEM((CHAN, 1, 128), F32),
            pltpu.VMEM((CHAN, 1, 128), F32),
            pltpu.VMEM((2 * LOCS, 256), BF),
            pltpu.VMEM((4, LOCS, BLOCK), BF),
            pltpu.VMEM((4, LOCS, BLOCK), BF),
            pltpu.VMEM((4, LOCS, BLOCK), F32),
            pltpu.VMEM((4, 128, BLOCK), BF),
            pltpu.VMEM((4, 128, BLOCK), BF),
            pltpu.VMEM((4, ZS, 8, BLOCK), BF),
            pltpu.VMEM((4, ZS, 8, BLOCK), F32),
            pltpu.VMEM((4, 2, 4, 8, BLOCK), BF),
            pltpu.VMEM((4, 2, 4, 8, BLOCK), BF),
            pltpu.VMEM((4, 2, 8, BLOCK), BF),
            pltpu.VMEM((8, 1024), F32),
            pltpu.VMEM((8, 128), F32),
            pltpu.VMEM((8, 128), F32),
            pltpu.VMEM((2, 2, ZS, 8, 1024), BF),
            dma((14,)),
            dma((1,)),
            dma((8,)),
            dma((8,)),
            dma((2,)),
            dma((2,)),
            dma((4,)),
            dma((4,)),
            dma((4,)),
            dma((2,)),
            dma((2, 4)),
            dma((4,)),
            dma((1,)),
            dma((3,)),
            dma((ZS,)),
            dma((ZS,)),
            dma((ZS,)),
            dma((ZS,)),
        ],
        compiler_params=pltpu.CompilerParams(
            collective_id=0, has_side_effects=True, vmem_limit_bytes=56 * 1024 * 1024
        ),
    )(
        pixels,
        patch_mask.T,
        embed_weight,
        mask_token.reshape(16, 128),
        chan_embed,
        agg_weight,
        group_map,
        group_map.reshape(1, C),
        query_key,
        group_bias,
        norm_gain.reshape(1, E),
        head_weight,
        head_bias,
    )


def solution(mesh):
    return jax.shard_map(
        shards,
        mesh=mesh,
        in_specs=(
            P("loc", "chan", None),
            P("loc", "chan"),
            P(),
            P(None, "loc"),
            P(),
            P("chan", None),
            P("chan"),
            P(),
            P(),
            P(),
            P(None, "chan", None),
            P("chan", None),
        ),
        out_specs=P("loc", "chan", None),
        check_vma=False,
    )
```

```python
import functools
import math

import jax
import jax.numpy as jnp
from jax import lax
from jax.experimental import pallas as pl
from jax.experimental.pallas import tpu as pltpu
from jax.sharding import PartitionSpec as P

C = 256
E = 2048
G = 64
H = 16
BUNDLE = 4
LOCS = 256
CHAN = 64
ZS = 16
BLOCK = 256
BF = jnp.bfloat16
F32 = jnp.float32
MESH = pl.DeviceIdType.MESH


def split(value, parts):
    pieces = []
    for _ in range(parts - 1):
        piece = value.astype(BF)
        pieces.append(piece)
        value = value - piece.astype(F32)
    return [*pieces, value.astype(BF)]


def exact_dot(onehot, value):
    return sum(jnp.dot(onehot, piece, preferred_element_type=F32) for piece in split(value, 3))


def kernel(
    pixels_h,
    mask_h,
    emb_h,
    token_h,
    ce_h,
    agg_h,
    map_h,
    gmv_h,
    qk_h,
    gbias_h,
    gain_h,
    head_h,
    hbias_h,
    out,
    raw,
    maskv,
    token,
    ce,
    agg,
    gm_s,
    gm_v,
    qk,
    gbias,
    gain,
    hraw,
    hbias,
    tokf,
    keep,
    px,
    wd,
    wg,
    b,
    pre,
    acc,
    expand,
    sbuf,
    rbuf,
    obuf,
    abuf,
    lhs,
    ps,
    pr,
    own,
    ys,
    yr,
    zs,
    zf,
    zr,
    rin,
    rout,
    pooled,
    ssb,
    ssr,
    jt,
    lsem,
    esem,
    rsem,
    psem,
    ssem,
    srsem,
    csem,
    crsem,
    yrsem,
    zsem,
    rinsem,
    zrsem,
    qrsem,
    jsem,
    jz,
    jy,
    jc,
    jd,
):
    ci = lax.axis_index("chan")
    li = lax.axis_index("loc")
    core = ci % 2
    z = (ci // 2) % ZS
    ylo = ci // (2 * ZS)
    x = li % 4
    yhi = li // 4
    way = 1 - 2 * core
    partner = ci + way
    ypartner = (ci + 2 * ZS) % CHAN
    nxt = yhi * 4 + (x + way + 4) % 4
    prv = yhi * 4 + (x - way + 4) % 4
    cross_loc = (1 - yhi) * 4 + x

    def at(chan, loc=None):
        return {"chan": chan, "loc": li if loc is None else loc}

    def rdma(src, dst, send, recv, where):
        return pltpu.make_async_remote_copy(
            src_ref=src, dst_ref=dst, send_sem=send, recv_sem=recv, device_id=where, device_id_type=MESH
        )

    def await_bytes(ref, sem):
        pltpu.make_async_copy(ref, ref, sem).wait()

    diagonals = [(1 - yhi) * 4 + n % 4 for n in (nxt, prv)]

    def load(k, src, dst):
        copy = pltpu.make_async_copy(src, dst, lsem.at[k])
        copy.start()
        return copy

    first_half = load(0, emb_h.at[pl.ds(0, 128)], wg.at[li, 0])
    other_half = load(1, emb_h.at[pl.ds(128, 128)], wg.at[li, 1])

    def for_peers(act):
        @pl.loop(0, ZS - 1)
        def _(e):
            off = 8 - (e % 2) * ((e + 1) // 2) + (1 - e % 2) * (e // 2)
            there = ((z + off) % ZS) * 2
            for side in (1 - ylo, ylo):
                for c in range(2):
                    act(side * 2 * ZS + there + c)

        act((1 - ylo) * 2 * ZS + z * 2)
        act((1 - ylo) * 2 * ZS + z * 2 + 1)
        act(partner)

    barrier = pltpu.get_barrier_semaphore()
    for chan, loc in ((ci, nxt), (ci, prv), (ypartner, cross_loc), *((ypartner, d) for d in diagonals)):
        pl.semaphore_signal(barrier, inc=1, device_id=at(chan, loc), device_id_type=MESH)
    for_peers(lambda p: pl.semaphore_signal(barrier, inc=1, device_id=at(p), device_id_type=MESH))
    loads = [
        load(2, pixels_h, raw),
        load(3, mask_h, maskv),
        load(4, token_h, token),
        load(5, ce_h, ce),
        load(6, agg_h, agg),
        load(7, map_h, gm_s),
        load(8, gmv_h, gm_v),
        load(9, qk_h, qk),
        load(10, gbias_h, gbias),
        load(11, gain_h, gain),
        load(12, hbias_h, hbias),
    ]
    heads = load(13, head_h, hraw)

    def place(t, row):
        return ((yhi + row) % 2) * 4 + (x + way * ((3 * t * t - 5 * t) // 2) + 8) % 4

    swapped = {1: 1, 2: 4, 3: 5, 4: 2, 5: 3, 6: 6, 7: 7}

    def half(step):
        return wg.at[place(step // 2, step % 2), core]

    def pass_on(step, to, loc):
        rdma(half(step), half(step), esem.at[0], rsem.at[to], at(ci, loc)).start()

    def to_partner(step):
        rdma(half(step), half(step), esem.at[0], psem.at[swapped[step]], at(partner)).start()

    def arrived(step):
        await_bytes(half(step), rsem.at[step])

    first_half.wait()
    other_half.wait()
    for copy in loads:
        copy.wait()

    base = ci * BUNDLE
    groups = [gm_s[base + k] for k in range(BUNDLE)]
    low = jnp.minimum(jnp.minimum(groups[0], groups[1]), jnp.minimum(groups[2], groups[3]))
    weights = []
    for k in range(BUNDLE):
        full = 0.5 * agg[k]
        second = jnp.where(groups[k] != low, full, 0.0)
        weights.append((full - second, second))

    acc[...] = jnp.zeros_like(acc)
    tokf[...] = token[...].astype(F32)

    @pl.loop(0, BUNDLE)
    def _(c):
        hid = jnp.broadcast_to(maskv[pl.ds(c, 1), :].astype(F32), (128, LOCS)).T
        rows = pl.ds(pl.multiple_of(c * LOCS, LOCS), LOCS)
        at_lane = lax.broadcasted_iota(jnp.int32, (LOCS, 128), 1)
        px[rows, BLOCK:] = jnp.where(at_lane == 0, hid, jnp.where(at_lane == 1 + c, 1.0, 0.0)).astype(BF)
        keep[c] = 1.0 - hid

    @pl.loop(0, LOCS // 32)
    def _(i):
        rows = pl.ds(pl.multiple_of(i * 32, 32), 32)
        turned = jnp.swapaxes(raw[rows], 0, 1)
        for c in range(BUNDLE):
            shown = keep[c, rows, :]
            kept = turned[c].astype(F32) * jnp.concatenate([shown, shown], axis=1)
            px[pl.ds(pl.multiple_of(c * LOCS + i * 32, 32), 32), 0:BLOCK] = kept.astype(BF)

    @pl.loop(0, 8)
    def _(step):
        p = lax.broadcasted_iota(jnp.int32, (BLOCK, BLOCK), 0) % H
        head = 2 * step + lax.broadcasted_iota(jnp.int32, (BLOCK, BLOCK), 1) // 128
        expand[step] = jnp.where(p == head, 1.0, 0.0).astype(BF)

    row16 = lax.broadcasted_iota(jnp.int32, (128, BLOCK), 0)

    def embed_block(j):
        columns = pl.ds(pl.multiple_of(j * BLOCK, BLOCK), BLOCK)
        hide = jnp.concatenate([tokf[pl.ds(2 * j, 1), :], tokf[pl.ds(2 * j + 1, 1), :]], axis=1)
        extra = jnp.where(row16 == 0, hide, 0.0)
        embeds = ce[:, columns].astype(F32)
        for k in range(BUNDLE):
            extra = jnp.where(row16 == 1 + k, embeds[k : k + 1], extra)
        weight = jnp.concatenate([wg[j].reshape(BLOCK, BLOCK), extra.astype(BF)], axis=0)
        pre[...] = jnp.dot(px[...], weight, preferred_element_type=F32)

        @pl.loop(0, LOCS // 32)
        def _(chunk):
            first, second = None, None
            for k in range(BUNDLE):
                v = pre[pl.ds(pl.multiple_of(k * LOCS + chunk * 32, 32), 32), :]
                g = v + v * lax.erf(v * (1.0 / math.sqrt(2.0)))
                w0, w1 = weights[k]
                first = g * w0 if first is None else first + g * w0
                second = g * w1 if second is None else second + g * w1
            b[j, pl.ds(pl.multiple_of(chunk * 32, 32), 32), :] = first.astype(BF)
            b[j, pl.ds(pl.multiple_of(LOCS + chunk * 32, 32), 32), :] = second.astype(BF)

        q = jnp.concatenate([qk[:, columns]] * 8, axis=0)
        acc[...] += lax.dot_general(b[j], q, (((1,), (1,)), ((), ())), preferred_element_type=F32)

    embed_block(li)
    pl.semaphore_wait(barrier, CHAN - 1 + 5)
    mine = wg.at[li, core]
    rdma(mine, mine, esem.at[0], rsem.at[2], at(ci, nxt)).start()
    rdma(mine, mine, esem.at[0], rsem.at[4], at(ci, prv)).start()
    rdma(mine, mine, esem.at[0], rsem.at[1], at(ypartner, cross_loc)).start()
    rdma(mine, mine, esem.at[0], rsem.at[3], at(ypartner, diagonals[0])).start()
    rdma(mine, mine, esem.at[0], rsem.at[5], at(ypartner, diagonals[1])).start()

    @pl.loop(1, 8)
    def _(step):
        @pl.when(step == 1)
        def _():
            arrived(2)
            pass_on(2, 6, nxt)
            to_partner(2)
            arrived(4)
            to_partner(4)

        @pl.when(step == 3)
        def _():
            arrived(1)
            to_partner(1)
            arrived(3)
            pass_on(3, 7, nxt)
            to_partner(3)
            arrived(6)
            to_partner(6)

        @pl.when(step == 4)
        def _():
            arrived(5)
            to_partner(5)

        @pl.when(step == 6)
        def _():
            arrived(7)
            to_partner(7)

        t, row = step % 4, step // 4
        j = place(t, row)
        await_bytes(wg.at[j, 1 - core], psem.at[2 * t + row])
        embed_block(j)

    lane = lax.broadcasted_iota(jnp.int32, (CHAN, 128), 1)
    part = jnp.zeros((CHAN, 128), F32)
    for q in range(8):
        part = part + jnp.where(lane // H == q, acc[q * 64 : (q + 1) * 64, :], 0.0)
    sbuf[:, 0, :] = part
    sbuf[:, 1, :] = jnp.concatenate([part[16:32], part[0:16], part[48:64], part[32:48]], axis=0)

    for_peers(lambda p: rdma(sbuf.at[p], rbuf.at[ci], ssem.at[0], srsem.at[0], at(p)).start())

    rbuf[ci] = sbuf[ci]
    gmap = jnp.broadcast_to(gm_v[...].astype(F32), (8, C))
    wide = lax.broadcasted_iota(jnp.int32, (CHAN, C), 1)
    bund = lax.broadcasted_iota(jnp.int32, (CHAN, C), 0)
    inside = wide // BUNDLE == bund
    lows = jnp.min(jnp.where(inside, gmap[0:1], 1e9), axis=1, keepdims=True)
    highs = jnp.max(jnp.where(inside, gmap[0:1], -1.0), axis=1, keepdims=True)
    gcol = lax.broadcasted_iota(jnp.int32, (CHAN, G), 1).astype(F32)
    from_group = [jnp.where(v == gcol, 1.0, 0.0).astype(BF) for v in (lows, highs)]
    to_group = [f.astype(F32).T.astype(BF) for f in from_group]

    bias = jnp.concatenate([gbias[...]] * 8, axis=0).T
    heads.wait()

    @pl.loop(0, E // 32)
    def _(i):
        rows = pl.ds(pl.multiple_of(i * 32, 32), 32)
        wd[:, rows, :] = jnp.swapaxes(hraw[rows], 0, 1)

    await_bytes(rbuf.at[pl.ds(0, CHAN - 1)], srsem.at[0])
    lane2 = lax.broadcasted_iota(jnp.int32, (CHAN, 256), 1) % 128
    got = jnp.concatenate([rbuf[:, 0, :], rbuf[:, 1, :]], axis=1)
    mixed = jnp.where(lane2 < 64, exact_dot(to_group[0], got), exact_dot(to_group[1], got))
    turned = [pltpu.roll(mixed[:, k * 128 : (k + 1) * 128], 64, 1) for k in range(2)]
    scores = mixed + jnp.concatenate(turned, axis=1) + jnp.concatenate([bias, bias], axis=1)
    top = jnp.max(scores, axis=0, keepdims=True)
    raised = jnp.exp(scores - top)
    attn = raised / jnp.sum(raised, axis=0, keepdims=True)
    back = jnp.where(lane2 < 64, exact_dot(from_group[0], attn), exact_dot(from_group[1], attn))
    upper = z >= ZS // 2
    obuf[:, 0, :] = jnp.where(upper, back[:, 128:], back[:, :128])
    obuf[:, 1, :] = jnp.where(upper, back[:, :128], back[:, 128:])
    pair = ylo * ZS + (z % (ZS // 2)) * 2 + core

    for off in (12, 3, 13, 2, 14, 1, 15):
        there = ((z + off) % ZS) * 2
        for side in (1 - ylo, ylo):
            for c in range(2):
                peer = side * 2 * ZS + there + c
                rdma(obuf.at[peer], abuf.at[pair], ssem.at[1], srsem.at[1], at(peer)).start()

    for peer in ((1 - ylo) * 2 * ZS + z * 2, (1 - ylo) * 2 * ZS + z * 2 + 1, partner):
        rdma(obuf.at[peer], abuf.at[pair], ssem.at[1], srsem.at[1], at(peer)).start()

    abuf[pair] = obuf[ci]
    await_bytes(abuf.at[pl.ds(0, 31)], srsem.at[1])
    low_sets, high_sets = abuf[:, 0, :], abuf[:, 1, :]
    received = jnp.concatenate([low_sets[0:16], high_sets[0:16], low_sets[16:32], high_sets[16:32]], axis=0)
    high, rest = split(received, 2)
    high, rest = high.astype(F32), rest.astype(F32)
    for q in range(8):
        lhs[q * 64 : (q + 1) * 64, 0:128] = jnp.where(lane // H == q, high, 0.0).astype(BF)
        lhs[q * 64 : (q + 1) * 64, 128:256] = jnp.where(lane // H == q, rest, 0.0).astype(BF)

    def weigh(j):
        spread = jnp.dot(lhs[...], expand[j], preferred_element_type=F32)
        return spread[:LOCS] * b[j, 0:LOCS, :].astype(F32) + spread[LOCS:] * b[j, LOCS:, :].astype(F32)

    @pl.loop(0, 4)
    def _(t):
        ps[t] = weigh((1 - core) * 4 + t).astype(BF)
        rdma(ps.at[t], pr.at[t], csem.at[0], crsem.at[t], at(partner)).start()

    @pl.loop(0, 4)
    def _(t):
        mixed_in = weigh(core * 4 + t)
        await_bytes(pr.at[t], crsem.at[t])
        own[t] = mixed_in + pr[t].astype(F32)
        theirs = pl.ds(pl.multiple_of((1 - ylo) * 128, 128), 128)
        ys[t] = own[t, theirs, :].astype(BF)
        rdma(ys.at[t], yr.at[t], csem.at[1], yrsem.at[t], at(ypartner)).start()

    def zdev(to):
        return at(ylo * 2 * ZS + to * 2 + core)

    @pl.loop(0, 4)
    def _(t):
        mine = pl.ds(pl.multiple_of(ylo * 128, 128), 128)
        await_bytes(yr.at[t], yrsem.at[t])
        total = own[t, mine, :] + yr[t].astype(F32)
        total = total.reshape(ZS, 8, BLOCK)
        zf[t] = total
        zs[t] = total.astype(BF)
        for d in (8, 7, 6, 5):
            to, via = (z + d) % ZS, (z + d - 4) % ZS
            rdma(zs.at[t, to], rin.at[t, 0, d - 5], zsem.at[0], rinsem.at[0, t], zdev(via)).start()
            if d < 8:
                to, via = (z + ZS - d) % ZS, (z + ZS - d + 4) % ZS
                rdma(zs.at[t, to], rin.at[t, 1, d - 5], zsem.at[0], rinsem.at[1, t], zdev(via)).start()
        for d in (3, 2, 1):
            for q, to in enumerate(((z + d) % ZS, (z + ZS - d) % ZS)):
                rdma(zs.at[t, to], zr.at[t, q, d - 1], zsem.at[0], zrsem.at[t], zdev(to)).start()

    @pl.loop(0, 4)
    def _(t):
        for q, to, n in ((0, (z + 4) % ZS, 4), (1, (z + ZS - 4) % ZS, 3)):
            await_bytes(rin.at[t, q, pl.ds(0, n)], rinsem.at[q, t])
            total = zf[t, to]
            for d in range(n):
                total = total + rin[t, q, d].astype(F32)
            rout[t, q] = total.astype(BF)
            rdma(rout.at[t, q], zr.at[t, q, 3], zsem.at[1], zrsem.at[t], zdev(to)).start()

    squares = jnp.zeros((8, 1), F32)
    for t in range(4):
        await_bytes(zr.at[t], zrsem.at[t])
        total = zf[t, z]
        for q in range(2):
            for d in range(4):
                total = total + zr[t, q, d].astype(F32)
        pooled[:, t * BLOCK : (t + 1) * BLOCK] = total
        squares = squares + jnp.sum(total * total, axis=1, keepdims=True)
    ssb[...] = jnp.broadcast_to(squares, (8, 128))
    share = rdma(ssb, ssr, csem.at[3], qrsem.at[0], at(partner))
    share.start()
    scaled = pooled[...] * gain[:, pl.ds(pl.multiple_of(core * 1024, 1024), 1024)]
    share.wait_recv()
    inverse = lax.rsqrt((squares + ssr[:, 0:1]) * (1.0 / E) + 1e-06)
    jt[core, ylo, z] = (scaled * inverse).astype(BF)

    def row_block(row, d):
        return jt.at[core, row, (z + ZS - d) % ZS]

    def spread(d, way_z, steps):
        for n in steps:
            block = row_block(ylo, d)
            there = (d + way_z * n) % ZS
            rdma(block, block, jsem.at[0], jz.at[there], zdev((z + ZS + way_z * n) % ZS)).start()

    def share_block(d):
        block = row_block(ylo, d)
        rdma(block, block, jsem.at[1], jy.at[d], at(ypartner)).start()
        rdma(block, block, jsem.at[2], jc.at[d], at(partner)).start()

    for n in (4, 3, 2, 1):
        spread(0, 1, (n,))
        spread(0, -1, (n,))
    share_block(0)
    order = (4, 12, 1, 15, 2, 14, 3, 13, 5, 11, 6, 10, 7, 9, 8)
    for d in order:
        await_bytes(row_block(ylo, d), jz.at[d])
        if d == 4:
            spread(4, 1, (4, 3, 2, 1))
        if d == 12:
            spread(12, -1, (3, 2, 1))
        share_block(d)
    def decode(row):
        sides = [jt[c, row].reshape(128, 1024) for c in range(2)]

        @pl.loop(0, BUNDLE)
        def _(c):
            total = jnp.dot(sides[0], wd[c, 0:1024, :], preferred_element_type=F32)
            total = total + jnp.dot(sides[1], wd[c, 1024:2048, :], preferred_element_type=F32)
            rows = pl.ds(pl.multiple_of(row * 128, 128), 128)
            columns = pl.ds(pl.multiple_of(c * BLOCK, BLOCK), BLOCK)
            out[rows, columns] = (total + hbias[pl.ds(c, 1), :]).astype(BF)

    for d in range(ZS):
        block = jt.at[1 - core, ylo, (z + ZS - d) % ZS]
        await_bytes(block, jc.at[d])
    decode(ylo)
    for d in (0, *order):
        block = row_block(1 - ylo, d)
        await_bytes(block, jy.at[d])
        rdma(block, block, jsem.at[2], jd.at[d], at(partner)).start()

    for d in range(ZS):
        block = jt.at[1 - core, 1 - ylo, (z + ZS - d) % ZS]
        await_bytes(block, jd.at[d])
    decode(1 - ylo)

    await_bytes(wg.at[pl.ds(0, 7)], esem.at[0])
    await_bytes(sbuf.at[pl.ds(0, CHAN - 1)], ssem.at[0])
    await_bytes(obuf.at[pl.ds(0, 31)], ssem.at[1])
    await_bytes(ps, csem.at[0])
    await_bytes(ys, csem.at[1])
    await_bytes(zs.at[:, pl.ds(0, 13)], zsem.at[0])
    await_bytes(rout, zsem.at[1])
    share.wait_send()
    await_bytes(jt.at[0, 0, pl.ds(0, ZS - 1)], jsem.at[0])
    await_bytes(jt.at[0, 0], jsem.at[1])
    await_bytes(jt.at[0], jsem.at[2])


def shards(
    pixels,
    patch_mask,
    group_map,
    embed_weight,
    mask_token,
    chan_embed,
    agg_weight,
    query_key,
    group_bias,
    norm_gain,
    head_weight,
    head_bias,
):
    vmem = pl.BlockSpec(memory_space=pltpu.VMEM)
    hbm = pl.BlockSpec(memory_space=pltpu.HBM)
    dma = pltpu.SemaphoreType.DMA
    decoded = pl.pallas_call(
        kernel,
        out_shape=jax.ShapeDtypeStruct((LOCS, BUNDLE * BLOCK), BF),
        in_specs=[hbm] * 13,
        out_specs=vmem,
        scratch_shapes=[
            pltpu.VMEM((LOCS, BUNDLE, BLOCK), BF),
            pltpu.VMEM((BUNDLE, LOCS), jnp.int32),
            pltpu.VMEM((16, 128), BF),
            pltpu.VMEM((BUNDLE, E), BF),
            pltpu.SMEM((BUNDLE,), F32),
            pltpu.SMEM((C,), jnp.int32),
            pltpu.VMEM((1, C), jnp.int32),
            pltpu.VMEM((H, E), BF),
            pltpu.VMEM((H, G), F32),
            pltpu.VMEM((1, E), F32),
            pltpu.VMEM((E, BUNDLE, BLOCK), BF),
            pltpu.VMEM((BUNDLE, BLOCK), F32),
            pltpu.VMEM((16, 128), F32),
            pltpu.VMEM((BUNDLE, LOCS, 128), F32),
            pltpu.VMEM((BUNDLE * LOCS, BLOCK + 128), BF),
            pltpu.VMEM((BUNDLE, E, BLOCK), BF),
            pltpu.VMEM((8, 2, 128, BLOCK), BF),
            pltpu.VMEM((8, 2 * LOCS, BLOCK), BF),
            pltpu.VMEM((BUNDLE * LOCS, BLOCK), F32),
            pltpu.VMEM((2 * LOCS, 128), F32),
            pltpu.VMEM((8, BLOCK, BLOCK), BF),
            pltpu.VMEM((CHAN, 2, 128), F32),
            pltpu.VMEM((CHAN, 2, 128), F32),
            pltpu.VMEM((CHAN, 2, 128), F32),
            pltpu.VMEM((CHAN // 2, 2, 128), F32),
            pltpu.VMEM((2 * LOCS, 256), BF),
            pltpu.VMEM((4, LOCS, BLOCK), BF),
            pltpu.VMEM((4, LOCS, BLOCK), BF),
            pltpu.VMEM((4, LOCS, BLOCK), F32),
            pltpu.VMEM((4, 128, BLOCK), BF),
            pltpu.VMEM((4, 128, BLOCK), BF),
            pltpu.VMEM((4, ZS, 8, BLOCK), BF),
            pltpu.VMEM((4, ZS, 8, BLOCK), F32),
            pltpu.VMEM((4, 2, 4, 8, BLOCK), BF),
            pltpu.VMEM((4, 2, 4, 8, BLOCK), BF),
            pltpu.VMEM((4, 2, 8, BLOCK), BF),
            pltpu.VMEM((8, 1024), F32),
            pltpu.VMEM((8, 128), F32),
            pltpu.VMEM((8, 128), F32),
            pltpu.VMEM((2, 2, ZS, 8, 1024), BF),
            dma((14,)),
            dma((1,)),
            dma((8,)),
            dma((8,)),
            dma((2,)),
            dma((2,)),
            dma((4,)),
            dma((4,)),
            dma((4,)),
            dma((2,)),
            dma((2, 4)),
            dma((4,)),
            dma((1,)),
            dma((3,)),
            dma((ZS,)),
            dma((ZS,)),
            dma((ZS,)),
            dma((ZS,)),
        ],
        compiler_params=pltpu.CompilerParams(
            collective_id=0, has_side_effects=True, vmem_limit_bytes=32 * 1024 * 1024
        ),
    )(*[pltpu.with_memory_space_constraint(v, pltpu.HBM) for v in (
        pixels,
        patch_mask.T,
        embed_weight,
        mask_token.reshape(16, 128),
        chan_embed,
        agg_weight,
        group_map,
        group_map.reshape(1, C),
        query_key,
        group_bias,
        norm_gain.reshape(1, E),
        head_weight,
        head_bias,
    )])
    return decoded.reshape(pixels.shape)


def solution(mesh):
    return jax.shard_map(
        shards,
        mesh=mesh,
        in_specs=(
            P("loc", "chan", None),
            P("loc", "chan"),
            P(),
            P(None, "loc"),
            P(),
            P("chan", None),
            P("chan"),
            P(),
            P(),
            P(),
            P(None, "chan", None),
            P("chan", None),
        ),
        out_specs=P("loc", "chan", None),
        check_vma=False,
    )
```

```python
import functools
import math

import jax
import jax.numpy as jnp
from jax import lax
from jax.experimental import pallas as pl
from jax.experimental.pallas import tpu as pltpu
from jax.sharding import PartitionSpec as P

C = 256
E = 2048
G = 64
H = 16
BUNDLE = 4
LOCS = 256
CHAN = 64
ZS = 16
BLOCK = 256
BF = jnp.bfloat16
F32 = jnp.float32
MESH = pl.DeviceIdType.MESH


def split(value, parts):
    pieces = []
    for _ in range(parts - 1):
        piece = value.astype(BF)
        pieces.append(piece)
        value = value - piece.astype(F32)
    return [*pieces, value.astype(BF)]


def exact_dot(onehot, value):
    return sum(jnp.dot(onehot, piece, preferred_element_type=F32) for piece in split(value, 3))


def kernel(
    pixels_h,
    mask_h,
    emb_h,
    token_h,
    ce_h,
    agg_h,
    map_h,
    gmv_h,
    qk_h,
    gbias_h,
    gain_h,
    head_h,
    hbias_h,
    out,
    raw,
    maskv,
    token,
    ce,
    agg,
    gm_s,
    gm_v,
    qk,
    gbias,
    gain,
    hraw,
    hbias,
    tokf,
    keep,
    px,
    wd,
    dec,
    wg,
    b,
    pre,
    acc,
    expand,
    sbuf,
    rbuf,
    obuf,
    abuf,
    lhs,
    ps,
    pr,
    own,
    ys,
    yr,
    zs,
    zf,
    zr,
    rin,
    rout,
    pooled,
    ssb,
    ssr,
    jt,
    lsem,
    esem,
    rsem,
    psem,
    ssem,
    srsem,
    csem,
    crsem,
    yrsem,
    zsem,
    rinsem,
    zrsem,
    qrsem,
    jsem,
    jz,
    jy,
    jc,
    jd,
):
    ci = lax.axis_index("chan")
    li = lax.axis_index("loc")
    core = ci % 2
    z = (ci // 2) % ZS
    ylo = ci // (2 * ZS)
    x = li % 4
    yhi = li // 4
    way = 1 - 2 * core
    partner = ci + way
    ypartner = (ci + 2 * ZS) % CHAN
    nxt = yhi * 4 + (x + way + 4) % 4
    prv = yhi * 4 + (x - way + 4) % 4
    cross_loc = (1 - yhi) * 4 + x

    def at(chan, loc=None):
        return {"chan": chan, "loc": li if loc is None else loc}

    def rdma(src, dst, send, recv, where):
        return pltpu.make_async_remote_copy(
            src_ref=src, dst_ref=dst, send_sem=send, recv_sem=recv, device_id=where, device_id_type=MESH
        )

    def await_bytes(ref, sem):
        pltpu.make_async_copy(ref, ref, sem).wait()

    diagonals = [(1 - yhi) * 4 + n % 4 for n in (nxt, prv)]

    def load(k, src, dst):
        copy = pltpu.make_async_copy(src, dst, lsem.at[k])
        copy.start()
        return copy

    first_half = load(0, emb_h.at[pl.ds(0, 128)], wg.at[li, 0])
    other_half = load(1, emb_h.at[pl.ds(128, 128)], wg.at[li, 1])

    def for_peers(act):
        @pl.loop(0, ZS - 1)
        def _(e):
            off = 8 - (e % 2) * ((e + 1) // 2) + (1 - e % 2) * (e // 2)
            there = ((z + off) % ZS) * 2
            for side in (1 - ylo, ylo):
                for c in range(2):
                    act(side * 2 * ZS + there + c)

        act((1 - ylo) * 2 * ZS + z * 2)
        act((1 - ylo) * 2 * ZS + z * 2 + 1)
        act(partner)

    barrier = pltpu.get_barrier_semaphore()
    for chan, loc in ((ci, nxt), (ci, prv), (ypartner, cross_loc), *((ypartner, d) for d in diagonals)):
        pl.semaphore_signal(barrier, inc=1, device_id=at(chan, loc), device_id_type=MESH)
    for_peers(lambda p: pl.semaphore_signal(barrier, inc=1, device_id=at(p), device_id_type=MESH))
    loads = [
        load(2, pixels_h, raw),
        load(3, mask_h, maskv),
        load(4, token_h, token),
        load(5, ce_h, ce),
        load(6, agg_h, agg),
        load(7, map_h, gm_s),
        load(8, gmv_h, gm_v),
        load(9, qk_h, qk),
        load(10, gbias_h, gbias),
        load(11, gain_h, gain),
        load(12, hbias_h, hbias),
    ]
    heads = load(13, head_h, hraw)

    def place(t, row):
        return ((yhi + row) % 2) * 4 + (x + way * ((3 * t * t - 5 * t) // 2) + 8) % 4

    swapped = {1: 1, 2: 4, 3: 5, 4: 2, 5: 3, 6: 6, 7: 7}

    def half(step):
        return wg.at[place(step // 2, step % 2), core]

    def pass_on(step, to, loc):
        rdma(half(step), half(step), esem.at[0], rsem.at[to], at(ci, loc)).start()

    def to_partner(step):
        rdma(half(step), half(step), esem.at[0], psem.at[swapped[step]], at(partner)).start()

    def arrived(step):
        await_bytes(half(step), rsem.at[step])

    first_half.wait()
    other_half.wait()
    for copy in loads:
        copy.wait()

    base = ci * BUNDLE
    groups = [gm_s[base + k] for k in range(BUNDLE)]
    low = jnp.minimum(jnp.minimum(groups[0], groups[1]), jnp.minimum(groups[2], groups[3]))
    weights = []
    for k in range(BUNDLE):
        full = 0.5 * agg[k]
        second = jnp.where(groups[k] != low, full, 0.0)
        weights.append((full - second, second))

    acc[...] = jnp.zeros_like(acc)
    tokf[...] = token[...].astype(F32)

    @pl.loop(0, BUNDLE)
    def _(c):
        hid = jnp.broadcast_to(maskv[pl.ds(c, 1), :].astype(F32), (128, LOCS)).T
        rows = pl.ds(pl.multiple_of(c * LOCS, LOCS), LOCS)
        at_lane = lax.broadcasted_iota(jnp.int32, (LOCS, 128), 1)
        px[rows, BLOCK:] = jnp.where(at_lane == 0, hid, jnp.where(at_lane == 1 + c, 1.0, 0.0)).astype(BF)
        keep[c] = 1.0 - hid

    @pl.loop(0, LOCS // 32)
    def _(i):
        rows = pl.ds(pl.multiple_of(i * 32, 32), 32)
        turned = jnp.swapaxes(raw[rows], 0, 1)
        for c in range(BUNDLE):
            shown = keep[c, rows, :]
            kept = turned[c].astype(F32) * jnp.concatenate([shown, shown], axis=1)
            px[pl.ds(pl.multiple_of(c * LOCS + i * 32, 32), 32), 0:BLOCK] = kept.astype(BF)

    @pl.loop(0, 8)
    def _(step):
        p = lax.broadcasted_iota(jnp.int32, (BLOCK, BLOCK), 0) % H
        head = 2 * step + lax.broadcasted_iota(jnp.int32, (BLOCK, BLOCK), 1) // 128
        expand[step] = jnp.where(p == head, 1.0, 0.0).astype(BF)

    row16 = lax.broadcasted_iota(jnp.int32, (128, BLOCK), 0)

    def embed_block(j):
        columns = pl.ds(pl.multiple_of(j * BLOCK, BLOCK), BLOCK)
        hide = jnp.concatenate([tokf[pl.ds(2 * j, 1), :], tokf[pl.ds(2 * j + 1, 1), :]], axis=1)
        extra = jnp.where(row16 == 0, hide, 0.0)
        embeds = ce[:, columns].astype(F32)
        for k in range(BUNDLE):
            extra = jnp.where(row16 == 1 + k, embeds[k : k + 1], extra)
        weight = jnp.concatenate([wg[j].reshape(BLOCK, BLOCK), extra.astype(BF)], axis=0)
        pre[...] = jnp.dot(px[...], weight, preferred_element_type=F32)

        @pl.loop(0, LOCS // 32)
        def _(chunk):
            first, second = None, None
            for k in range(BUNDLE):
                v = pre[pl.ds(pl.multiple_of(k * LOCS + chunk * 32, 32), 32), :]
                g = v + v * lax.erf(v * (1.0 / math.sqrt(2.0)))
                w0, w1 = weights[k]
                first = g * w0 if first is None else first + g * w0
                second = g * w1 if second is None else second + g * w1
            b[j, pl.ds(pl.multiple_of(chunk * 32, 32), 32), :] = first.astype(BF)
            b[j, pl.ds(pl.multiple_of(LOCS + chunk * 32, 32), 32), :] = second.astype(BF)

        q = jnp.concatenate([qk[:, columns]] * 8, axis=0)
        acc[...] += lax.dot_general(b[j], q, (((1,), (1,)), ((), ())), preferred_element_type=F32)

    embed_block(li)
    pl.semaphore_wait(barrier, CHAN - 1 + 5)
    mine = wg.at[li, core]
    rdma(mine, mine, esem.at[0], rsem.at[2], at(ci, nxt)).start()
    rdma(mine, mine, esem.at[0], rsem.at[4], at(ci, prv)).start()
    rdma(mine, mine, esem.at[0], rsem.at[1], at(ypartner, cross_loc)).start()

    @pl.loop(1, 8)
    def _(step):
        @pl.when(step == 1)
        def _():
            arrived(2)
            pass_on(2, 6, nxt)
            to_partner(2)
            arrived(4)
            to_partner(4)
            rdma(mine, mine, esem.at[0], rsem.at[3], at(ypartner, diagonals[0])).start()
            rdma(mine, mine, esem.at[0], rsem.at[5], at(ypartner, diagonals[1])).start()

        @pl.when(step == 3)
        def _():
            arrived(6)
            to_partner(6)
            arrived(1)
            to_partner(1)

        @pl.when(step == 4)
        def _():
            arrived(3)
            pass_on(3, 7, nxt)
            to_partner(3)

        @pl.when(step == 5)
        def _():
            arrived(5)
            to_partner(5)

        @pl.when(step == 6)
        def _():
            arrived(7)
            to_partner(7)

        t, row = step % 4, step // 4
        j = place(t, row)
        await_bytes(wg.at[j, 1 - core], psem.at[2 * t + row])
        embed_block(j)

    lane = lax.broadcasted_iota(jnp.int32, (CHAN, 128), 1)
    part = jnp.zeros((CHAN, 128), F32)
    for q in range(8):
        part = part + jnp.where(lane // H == q, acc[q * 64 : (q + 1) * 64, :], 0.0)
    sbuf[:, 0, :] = part
    sbuf[:, 1, :] = jnp.concatenate([part[16:32], part[0:16], part[48:64], part[32:48]], axis=0)

    for_peers(lambda p: rdma(sbuf.at[p], rbuf.at[ci], ssem.at[0], srsem.at[0], at(p)).start())

    rbuf[ci] = sbuf[ci]
    gmap = jnp.broadcast_to(gm_v[...].astype(F32), (8, C))
    wide = lax.broadcasted_iota(jnp.int32, (CHAN, C), 1)
    bund = lax.broadcasted_iota(jnp.int32, (CHAN, C), 0)
    inside = wide // BUNDLE == bund
    lows = jnp.min(jnp.where(inside, gmap[0:1], 1e9), axis=1, keepdims=True)
    highs = jnp.max(jnp.where(inside, gmap[0:1], -1.0), axis=1, keepdims=True)
    gcol = lax.broadcasted_iota(jnp.int32, (CHAN, G), 1).astype(F32)
    from_group = [jnp.where(v == gcol, 1.0, 0.0).astype(BF) for v in (lows, highs)]
    to_group = [f.astype(F32).T.astype(BF) for f in from_group]

    bias = jnp.concatenate([gbias[...]] * 8, axis=0).T
    heads.wait()

    @pl.loop(0, E // 32)
    def _(i):
        rows = pl.ds(pl.multiple_of(i * 32, 32), 32)
        wd[:, rows, :] = jnp.swapaxes(hraw[rows], 0, 1)

    await_bytes(rbuf.at[pl.ds(0, CHAN - 1)], srsem.at[0])
    lane2 = lax.broadcasted_iota(jnp.int32, (CHAN, 256), 1) % 128
    got = jnp.concatenate([rbuf[:, 0, :], rbuf[:, 1, :]], axis=1)
    mixed = jnp.where(lane2 < 64, exact_dot(to_group[0], got), exact_dot(to_group[1], got))
    turned = [pltpu.roll(mixed[:, k * 128 : (k + 1) * 128], 64, 1) for k in range(2)]
    scores = mixed + jnp.concatenate(turned, axis=1) + jnp.concatenate([bias, bias], axis=1)
    top = jnp.max(scores, axis=0, keepdims=True)
    raised = jnp.exp(scores - top)
    attn = raised / jnp.sum(raised, axis=0, keepdims=True)
    back = jnp.where(lane2 < 64, exact_dot(from_group[0], attn), exact_dot(from_group[1], attn))
    upper = z >= ZS // 2
    obuf[:, 0, :] = jnp.where(upper, back[:, 128:], back[:, :128])
    obuf[:, 1, :] = jnp.where(upper, back[:, :128], back[:, 128:])
    pair = ylo * ZS + (z % (ZS // 2)) * 2 + core

    for off in (12, 3, 13, 2, 14, 1, 15):
        there = ((z + off) % ZS) * 2
        for side in (1 - ylo, ylo):
            for c in range(2):
                peer = side * 2 * ZS + there + c
                rdma(obuf.at[peer], abuf.at[pair], ssem.at[1], srsem.at[1], at(peer)).start()

    for peer in ((1 - ylo) * 2 * ZS + z * 2, (1 - ylo) * 2 * ZS + z * 2 + 1, partner):
        rdma(obuf.at[peer], abuf.at[pair], ssem.at[1], srsem.at[1], at(peer)).start()

    abuf[pair] = obuf[ci]
    await_bytes(abuf.at[pl.ds(0, 31)], srsem.at[1])
    low_sets, high_sets = abuf[:, 0, :], abuf[:, 1, :]
    received = jnp.concatenate([low_sets[0:16], high_sets[0:16], low_sets[16:32], high_sets[16:32]], axis=0)
    high, rest = split(received, 2)
    high, rest = high.astype(F32), rest.astype(F32)
    for q in range(8):
        lhs[q * 64 : (q + 1) * 64, 0:128] = jnp.where(lane // H == q, high, 0.0).astype(BF)
        lhs[q * 64 : (q + 1) * 64, 128:256] = jnp.where(lane // H == q, rest, 0.0).astype(BF)

    def weigh(j):
        spread = jnp.dot(lhs[...], expand[j], preferred_element_type=F32)
        return spread[:LOCS] * b[j, 0:LOCS, :].astype(F32) + spread[LOCS:] * b[j, LOCS:, :].astype(F32)

    @pl.loop(0, 4)
    def _(t):
        ps[t] = weigh((1 - core) * 4 + t).astype(BF)
        rdma(ps.at[t], pr.at[t], csem.at[0], crsem.at[t], at(partner)).start()

    @pl.loop(0, 4)
    def _(t):
        mixed_in = weigh(core * 4 + t)
        await_bytes(pr.at[t], crsem.at[t])
        own[t] = mixed_in + pr[t].astype(F32)
        theirs = pl.ds(pl.multiple_of((1 - ylo) * 128, 128), 128)
        ys[t] = own[t, theirs, :].astype(BF)
        rdma(ys.at[t], yr.at[t], csem.at[1], yrsem.at[t], at(ypartner)).start()

    def zdev(to):
        return at(ylo * 2 * ZS + to * 2 + core)

    def ahead(n):
        return (z + way * n + ZS) % ZS

    @pl.loop(0, 4)
    def _(t):
        mine = pl.ds(pl.multiple_of(ylo * 128, 128), 128)
        await_bytes(yr.at[t], yrsem.at[t])
        total = own[t, mine, :] + yr[t].astype(F32)
        total = total.reshape(ZS, 8, BLOCK)
        zf[t] = total
        zs[t] = total.astype(BF)
        for d in (8, 7, 6, 5):
            to, via = ahead(d), ahead(d - 4)
            rdma(zs.at[t, to], rin.at[t, 0, d - 5], zsem.at[0], rinsem.at[0, t], zdev(via)).start()
            if d < 8:
                to, via = ahead(-d), ahead(4 - d)
                rdma(zs.at[t, to], rin.at[t, 1, d - 5], zsem.at[0], rinsem.at[1, t], zdev(via)).start()
        for d in (3, 2, 1):
            for q, to in enumerate((ahead(d), ahead(-d))):
                rdma(zs.at[t, to], zr.at[t, q, d - 1], zsem.at[0], zrsem.at[t], zdev(to)).start()

    @pl.loop(0, 4)
    def _(t):
        for q, to, n in ((0, ahead(4), 4), (1, ahead(-4), 3)):
            await_bytes(rin.at[t, q, pl.ds(0, n)], rinsem.at[q, t])
            total = zf[t, to]
            for d in range(n):
                total = total + rin[t, q, d].astype(F32)
            rout[t, q] = total.astype(BF)
            rdma(rout.at[t, q], zr.at[t, q, 3], zsem.at[1], zrsem.at[t], zdev(to)).start()

    squares = jnp.zeros((8, 1), F32)
    for t in range(4):
        await_bytes(zr.at[t], zrsem.at[t])
        total = zf[t, z]
        for q in range(2):
            for d in range(4):
                total = total + zr[t, q, d].astype(F32)
        pooled[:, t * BLOCK : (t + 1) * BLOCK] = total
        squares = squares + jnp.sum(total * total, axis=1, keepdims=True)
    ssb[...] = jnp.broadcast_to(squares, (8, 128))
    share = rdma(ssb, ssr, csem.at[3], qrsem.at[0], at(partner))
    share.start()
    scaled = pooled[...] * gain[:, pl.ds(pl.multiple_of(core * 1024, 1024), 1024)]
    share.wait_recv()
    inverse = lax.rsqrt((squares + ssr[:, 0:1]) * (1.0 / E) + 1e-06)
    jt[core, ylo, z] = (scaled * inverse).astype(BF)

    def row_block(row, d):
        return jt.at[core, row, ahead(-d)]

    def spread(d, way_z, steps):
        for n in steps:
            block = row_block(ylo, d)
            there = (d + way_z * n) % ZS
            rdma(block, block, jsem.at[0], jz.at[there], zdev(ahead(way_z * n))).start()

    def share_block(d):
        block = row_block(ylo, d)
        rdma(block, block, jsem.at[1], jy.at[d], at(ypartner)).start()
        rdma(block, block, jsem.at[2], jc.at[d], at(partner)).start()

    for n in (4, 3, 2, 1):
        spread(0, 1, (n,))
        spread(0, -1, (n,))
    share_block(0)
    order = (4, 12, 1, 15, 2, 14, 3, 13, 5, 11, 6, 10, 7, 9, 8)
    for d in order:
        await_bytes(row_block(ylo, d), jz.at[d])
        if d == 4:
            spread(4, 1, (4, 3, 2, 1))
        if d == 12:
            spread(12, -1, (3, 2, 1))
        share_block(d)
    def decode_own(row):
        side = jt[core, row].reshape(128, 1024)

        @pl.loop(0, BUNDLE)
        def _(c):
            part = wd[c, pl.ds(pl.multiple_of(core * 1024, 1024), 1024), :]
            dec[c] = jnp.dot(side, part, preferred_element_type=F32) + hbias[pl.ds(c, 1), :]

    def decode_rest(row):
        side = jt[1 - core, row].reshape(128, 1024)

        @pl.loop(0, BUNDLE)
        def _(c):
            part = wd[c, pl.ds(pl.multiple_of((1 - core) * 1024, 1024), 1024), :]
            rows = pl.ds(pl.multiple_of(row * 128, 128), 128)
            columns = pl.ds(pl.multiple_of(c * BLOCK, BLOCK), BLOCK)
            out[rows, columns] = (dec[c] + jnp.dot(side, part, preferred_element_type=F32)).astype(BF)

    decode_own(ylo)
    for d in range(ZS):
        await_bytes(jt.at[1 - core, ylo, ahead(d)], jc.at[d])
    decode_rest(ylo)
    for d in (0, *order):
        block = row_block(1 - ylo, d)
        await_bytes(block, jy.at[d])
        rdma(block, block, jsem.at[2], jd.at[d], at(partner)).start()
    decode_own(1 - ylo)
    for d in range(ZS):
        await_bytes(jt.at[1 - core, 1 - ylo, ahead(d)], jd.at[d])
    decode_rest(1 - ylo)

    await_bytes(wg.at[pl.ds(0, 7)], esem.at[0])
    await_bytes(sbuf.at[pl.ds(0, CHAN - 1)], ssem.at[0])
    await_bytes(obuf.at[pl.ds(0, 31)], ssem.at[1])
    await_bytes(ps, csem.at[0])
    await_bytes(ys, csem.at[1])
    await_bytes(zs.at[:, pl.ds(0, 13)], zsem.at[0])
    await_bytes(rout, zsem.at[1])
    share.wait_send()
    await_bytes(jt.at[0, 0, pl.ds(0, ZS - 1)], jsem.at[0])
    await_bytes(jt.at[0, 0], jsem.at[1])
    await_bytes(jt.at[0], jsem.at[2])


def shards(
    pixels,
    patch_mask,
    group_map,
    embed_weight,
    mask_token,
    chan_embed,
    agg_weight,
    query_key,
    group_bias,
    norm_gain,
    head_weight,
    head_bias,
):
    vmem = pl.BlockSpec(memory_space=pltpu.VMEM)
    hbm = pl.BlockSpec(memory_space=pltpu.HBM)
    dma = pltpu.SemaphoreType.DMA
    decoded = pl.pallas_call(
        kernel,
        out_shape=jax.ShapeDtypeStruct((LOCS, BUNDLE * BLOCK), BF),
        in_specs=[hbm] * 13,
        out_specs=vmem,
        scratch_shapes=[
            pltpu.VMEM((LOCS, BUNDLE, BLOCK), BF),
            pltpu.VMEM((BUNDLE, LOCS), jnp.int32),
            pltpu.VMEM((16, 128), BF),
            pltpu.VMEM((BUNDLE, E), BF),
            pltpu.SMEM((BUNDLE,), F32),
            pltpu.SMEM((C,), jnp.int32),
            pltpu.VMEM((1, C), jnp.int32),
            pltpu.VMEM((H, E), BF),
            pltpu.VMEM((H, G), F32),
            pltpu.VMEM((1, E), F32),
            pltpu.VMEM((E, BUNDLE, BLOCK), BF),
            pltpu.VMEM((BUNDLE, BLOCK), F32),
            pltpu.VMEM((16, 128), F32),
            pltpu.VMEM((BUNDLE, LOCS, 128), F32),
            pltpu.VMEM((BUNDLE * LOCS, BLOCK + 128), BF),
            pltpu.VMEM((BUNDLE, E, BLOCK), BF),
            pltpu.VMEM((BUNDLE, 128, BLOCK), F32),
            pltpu.VMEM((8, 2, 128, BLOCK), BF),
            pltpu.VMEM((8, 2 * LOCS, BLOCK), BF),
            pltpu.VMEM((BUNDLE * LOCS, BLOCK), F32),
            pltpu.VMEM((2 * LOCS, 128), F32),
            pltpu.VMEM((8, BLOCK, BLOCK), BF),
            pltpu.VMEM((CHAN, 2, 128), F32),
            pltpu.VMEM((CHAN, 2, 128), F32),
            pltpu.VMEM((CHAN, 2, 128), F32),
            pltpu.VMEM((CHAN // 2, 2, 128), F32),
            pltpu.VMEM((2 * LOCS, 256), BF),
            pltpu.VMEM((4, LOCS, BLOCK), BF),
            pltpu.VMEM((4, LOCS, BLOCK), BF),
            pltpu.VMEM((4, LOCS, BLOCK), F32),
            pltpu.VMEM((4, 128, BLOCK), BF),
            pltpu.VMEM((4, 128, BLOCK), BF),
            pltpu.VMEM((4, ZS, 8, BLOCK), BF),
            pltpu.VMEM((4, ZS, 8, BLOCK), F32),
            pltpu.VMEM((4, 2, 4, 8, BLOCK), BF),
            pltpu.VMEM((4, 2, 4, 8, BLOCK), BF),
            pltpu.VMEM((4, 2, 8, BLOCK), BF),
            pltpu.VMEM((8, 1024), F32),
            pltpu.VMEM((8, 128), F32),
            pltpu.VMEM((8, 128), F32),
            pltpu.VMEM((2, 2, ZS, 8, 1024), BF),
            dma((14,)),
            dma((1,)),
            dma((8,)),
            dma((8,)),
            dma((2,)),
            dma((2,)),
            dma((4,)),
            dma((4,)),
            dma((4,)),
            dma((2,)),
            dma((2, 4)),
            dma((4,)),
            dma((1,)),
            dma((3,)),
            dma((ZS,)),
            dma((ZS,)),
            dma((ZS,)),
            dma((ZS,)),
        ],
        compiler_params=pltpu.CompilerParams(
            collective_id=0, has_side_effects=True, vmem_limit_bytes=32 * 1024 * 1024
        ),
    )(*[pltpu.with_memory_space_constraint(v, pltpu.HBM) for v in (
        pixels,
        patch_mask.T,
        embed_weight,
        mask_token.reshape(16, 128),
        chan_embed,
        agg_weight,
        group_map,
        group_map.reshape(1, C),
        query_key,
        group_bias,
        norm_gain.reshape(1, E),
        head_weight,
        head_bias,
    )])
    return decoded.reshape(pixels.shape)


def solution(mesh):
    return jax.shard_map(
        shards,
        mesh=mesh,
        in_specs=(
            P("loc", "chan", None),
            P("loc", "chan"),
            P(),
            P(None, "loc"),
            P(),
            P("chan", None),
            P("chan"),
            P(),
            P(),
            P(),
            P(None, "chan", None),
            P("chan", None),
        ),
        out_specs=P("loc", "chan", None),
        check_vma=False,
    )
```

```python
import functools
import math

import jax
import jax.numpy as jnp
from jax import lax
from jax.experimental import pallas as pl
from jax.experimental.pallas import tpu as pltpu
from jax.sharding import PartitionSpec as P

C = 256
E = 2048
G = 64
H = 16
BUNDLE = 4
LOCS = 256
CHAN = 64
ZS = 16
BLOCK = 256
BF = jnp.bfloat16
F32 = jnp.float32
MESH = pl.DeviceIdType.MESH


def split(value, parts):
    pieces = []
    for _ in range(parts - 1):
        piece = value.astype(BF)
        pieces.append(piece)
        value = value - piece.astype(F32)
    return [*pieces, value.astype(BF)]


def exact_dot(onehot, value):
    return sum(jnp.dot(onehot, piece, preferred_element_type=F32) for piece in split(value, 3))


def kernel(
    pixels_h,
    mask_h,
    emb_h,
    token_h,
    ce_h,
    agg_h,
    map_h,
    gmv_h,
    qk_h,
    gbias_h,
    gain_h,
    head_h,
    hbias_h,
    out,
    raw,
    maskv,
    token,
    ce,
    agg,
    gm_s,
    gm_v,
    qk,
    gbias,
    gain,
    hraw,
    hbias,
    tokf,
    keep,
    px,
    wd,
    dec,
    wg,
    b,
    pre,
    acc,
    expand,
    sbuf,
    rbuf,
    obuf,
    abuf,
    lhs,
    ps,
    pr,
    own,
    ys,
    yr,
    zs,
    zf,
    zr,
    rin,
    rout,
    pooled,
    ssb,
    ssr,
    jt,
    lsem,
    esem,
    rsem,
    psem,
    ssem,
    srsem,
    csem,
    crsem,
    yrsem,
    zsem,
    rinsem,
    zrsem,
    qrsem,
    jsem,
    jz,
    jy,
    jc,
    jd,
):
    ci = lax.axis_index("chan")
    li = lax.axis_index("loc")
    core = ci % 2
    z = (ci // 2) % ZS
    ylo = ci // (2 * ZS)
    x = li % 4
    yhi = li // 4
    way = 1 - 2 * core
    partner = ci + way
    ypartner = (ci + 2 * ZS) % CHAN
    nxt = yhi * 4 + (x + way + 4) % 4
    prv = yhi * 4 + (x - way + 4) % 4
    cross_loc = (1 - yhi) * 4 + x

    def at(chan, loc=None):
        return {"chan": chan, "loc": li if loc is None else loc}

    def rdma(src, dst, send, recv, where):
        return pltpu.make_async_remote_copy(
            src_ref=src, dst_ref=dst, send_sem=send, recv_sem=recv, device_id=where, device_id_type=MESH
        )

    def await_bytes(ref, sem):
        pltpu.make_async_copy(ref, ref, sem).wait()

    diagonals = [(1 - yhi) * 4 + n % 4 for n in (nxt, prv)]

    def load(k, src, dst):
        copy = pltpu.make_async_copy(src, dst, lsem.at[k])
        copy.start()
        return copy

    first_half = load(0, emb_h.at[pl.ds(0, 128)], wg.at[li, 0])
    other_half = load(1, emb_h.at[pl.ds(128, 128)], wg.at[li, 1])

    def for_peers(act):
        @pl.loop(0, ZS - 1)
        def _(e):
            off = 8 - (e % 2) * ((e + 1) // 2) + (1 - e % 2) * (e // 2)
            there = ((z + off) % ZS) * 2
            for side in (1 - ylo, ylo):
                for c in range(2):
                    act(side * 2 * ZS + there + c)

        act((1 - ylo) * 2 * ZS + z * 2)
        act((1 - ylo) * 2 * ZS + z * 2 + 1)
        act(partner)

    barrier = pltpu.get_barrier_semaphore()
    for chan, loc in ((ci, nxt), (ci, prv), (ypartner, cross_loc), *((ypartner, d) for d in diagonals)):
        pl.semaphore_signal(barrier, inc=1, device_id=at(chan, loc), device_id_type=MESH)
    for_peers(lambda p: pl.semaphore_signal(barrier, inc=1, device_id=at(p), device_id_type=MESH))
    loads = [
        load(2, pixels_h, raw),
        load(3, mask_h, maskv),
        load(4, token_h, token),
        load(5, ce_h, ce),
        load(6, agg_h, agg),
        load(7, map_h, gm_s),
        load(8, gmv_h, gm_v),
        load(9, qk_h, qk),
        load(10, gbias_h, gbias),
        load(11, gain_h, gain),
        load(12, hbias_h, hbias),
    ]
    heads = load(13, head_h, hraw)

    def place(t, row):
        return ((yhi + row) % 2) * 4 + (x + way * ((3 * t * t - 5 * t) // 2) + 8) % 4

    swapped = {1: 1, 2: 4, 3: 5, 4: 2, 5: 3, 6: 6, 7: 7}

    def half(step):
        return wg.at[place(step // 2, step % 2), core]

    def pass_on(step, to, loc):
        rdma(half(step), half(step), esem.at[0], rsem.at[to], at(ci, loc)).start()

    def to_partner(step):
        rdma(half(step), half(step), esem.at[0], psem.at[swapped[step]], at(partner)).start()

    def arrived(step):
        await_bytes(half(step), rsem.at[step])

    first_half.wait()
    other_half.wait()
    for copy in loads:
        copy.wait()

    base = ci * BUNDLE
    groups = [gm_s[base + k] for k in range(BUNDLE)]
    low = jnp.minimum(jnp.minimum(groups[0], groups[1]), jnp.minimum(groups[2], groups[3]))
    weights = []
    for k in range(BUNDLE):
        full = 0.5 * agg[k]
        second = jnp.where(groups[k] != low, full, 0.0)
        weights.append((full - second, second))

    acc[...] = jnp.zeros_like(acc)
    tokf[...] = token[...].astype(F32)

    @pl.loop(0, BUNDLE)
    def _(c):
        hid = jnp.broadcast_to(maskv[pl.ds(c, 1), :].astype(F32), (128, LOCS)).T
        rows = pl.ds(pl.multiple_of(c * LOCS, LOCS), LOCS)
        at_lane = lax.broadcasted_iota(jnp.int32, (LOCS, 128), 1)
        px[rows, BLOCK:] = jnp.where(at_lane == 0, hid, jnp.where(at_lane == 1 + c, 1.0, 0.0)).astype(BF)
        keep[c] = 1.0 - hid

    @pl.loop(0, LOCS // 32)
    def _(i):
        rows = pl.ds(pl.multiple_of(i * 32, 32), 32)
        turned = jnp.swapaxes(raw[rows], 0, 1)
        for c in range(BUNDLE):
            shown = keep[c, rows, :]
            kept = turned[c].astype(F32) * jnp.concatenate([shown, shown], axis=1)
            px[pl.ds(pl.multiple_of(c * LOCS + i * 32, 32), 32), 0:BLOCK] = kept.astype(BF)

    @pl.loop(0, 8)
    def _(step):
        p = lax.broadcasted_iota(jnp.int32, (BLOCK, BLOCK), 0) % H
        head = 2 * step + lax.broadcasted_iota(jnp.int32, (BLOCK, BLOCK), 1) // 128
        expand[step] = jnp.where(p == head, 1.0, 0.0).astype(BF)

    row16 = lax.broadcasted_iota(jnp.int32, (128, BLOCK), 0)

    def embed_block(j):
        columns = pl.ds(pl.multiple_of(j * BLOCK, BLOCK), BLOCK)
        hide = jnp.concatenate([tokf[pl.ds(2 * j, 1), :], tokf[pl.ds(2 * j + 1, 1), :]], axis=1)
        extra = jnp.where(row16 == 0, hide, 0.0)
        embeds = ce[:, columns].astype(F32)
        for k in range(BUNDLE):
            extra = jnp.where(row16 == 1 + k, embeds[k : k + 1], extra)
        weight = jnp.concatenate([wg[j].reshape(BLOCK, BLOCK), extra.astype(BF)], axis=0)
        pre[...] = jnp.dot(px[...], weight, preferred_element_type=F32)

        @pl.loop(0, LOCS // 32, unroll=True)
        def _(chunk):
            first, second = None, None
            for k in range(BUNDLE):
                v = pre[pl.ds(pl.multiple_of(k * LOCS + chunk * 32, 32), 32), :]
                g = v + v * lax.erf(v * (1.0 / math.sqrt(2.0)))
                w0, w1 = weights[k]
                first = g * w0 if first is None else first + g * w0
                second = g * w1 if second is None else second + g * w1
            b[j, pl.ds(pl.multiple_of(chunk * 32, 32), 32), :] = first.astype(BF)
            b[j, pl.ds(pl.multiple_of(LOCS + chunk * 32, 32), 32), :] = second.astype(BF)

        q = jnp.concatenate([qk[:, columns]] * 8, axis=0)
        acc[...] += lax.dot_general(b[j], q, (((1,), (1,)), ((), ())), preferred_element_type=F32)

    embed_block(li)
    pl.semaphore_wait(barrier, CHAN - 1 + 5)
    mine = wg.at[li, core]
    rdma(mine, mine, esem.at[0], rsem.at[2], at(ci, nxt)).start()
    rdma(mine, mine, esem.at[0], rsem.at[4], at(ci, prv)).start()
    rdma(mine, mine, esem.at[0], rsem.at[1], at(ypartner, cross_loc)).start()
    rdma(mine, mine, esem.at[0], rsem.at[3], at(ypartner, diagonals[0])).start()

    @pl.loop(1, 8)
    def _(step):
        @pl.when(step == 1)
        def _():
            arrived(2)
            pass_on(2, 6, nxt)
            to_partner(2)
            arrived(4)
            to_partner(4)
            rdma(mine, mine, esem.at[0], rsem.at[5], at(ypartner, diagonals[1])).start()

        @pl.when(step == 2)
        def _():
            arrived(1)
            to_partner(1)

        @pl.when(step == 3)
        def _():
            arrived(3)
            pass_on(3, 7, nxt)
            to_partner(3)
            arrived(6)
            to_partner(6)

        @pl.when(step == 4)
        def _():
            arrived(5)
            to_partner(5)

        @pl.when(step == 6)
        def _():
            arrived(7)
            to_partner(7)

        third = ((step // 3) % 2) * (1 - (step % 3 + 1) // 2)
        fourth = (step // 4) * (1 - (step % 4 + 3) // 4)
        turn = step + third - fourth
        t, row = turn % 4, turn // 4
        j = place(t, row)
        await_bytes(wg.at[j, 1 - core], psem.at[2 * t + row])
        embed_block(j)

    lane = lax.broadcasted_iota(jnp.int32, (CHAN, 128), 1)
    part = jnp.zeros((CHAN, 128), F32)
    for q in range(8):
        part = part + jnp.where(lane // H == q, acc[q * 64 : (q + 1) * 64, :], 0.0)
    sbuf[:, 0, :] = part
    sbuf[:, 1, :] = jnp.concatenate([part[16:32], part[0:16], part[48:64], part[32:48]], axis=0)

    for_peers(lambda p: rdma(sbuf.at[p], rbuf.at[ci], ssem.at[0], srsem.at[0], at(p)).start())

    rbuf[ci] = sbuf[ci]
    gmap = jnp.broadcast_to(gm_v[...].astype(F32), (8, C))
    wide = lax.broadcasted_iota(jnp.int32, (CHAN, C), 1)
    bund = lax.broadcasted_iota(jnp.int32, (CHAN, C), 0)
    inside = wide // BUNDLE == bund
    lows = jnp.min(jnp.where(inside, gmap[0:1], 1e9), axis=1, keepdims=True)
    highs = jnp.max(jnp.where(inside, gmap[0:1], -1.0), axis=1, keepdims=True)
    gcol = lax.broadcasted_iota(jnp.int32, (CHAN, G), 1).astype(F32)
    from_group = [jnp.where(v == gcol, 1.0, 0.0).astype(BF) for v in (lows, highs)]
    to_group = [f.astype(F32).T.astype(BF) for f in from_group]

    bias = jnp.concatenate([gbias[...]] * 8, axis=0).T
    heads.wait()

    @pl.loop(0, E // 32)
    def _(i):
        rows = pl.ds(pl.multiple_of(i * 32, 32), 32)
        wd[:, rows, :] = jnp.swapaxes(hraw[rows], 0, 1)

    await_bytes(rbuf.at[pl.ds(0, CHAN - 1)], srsem.at[0])
    lane2 = lax.broadcasted_iota(jnp.int32, (CHAN, 256), 1) % 128
    got = jnp.concatenate([rbuf[:, 0, :], rbuf[:, 1, :]], axis=1)
    mixed = jnp.where(lane2 < 64, exact_dot(to_group[0], got), exact_dot(to_group[1], got))
    turned = [pltpu.roll(mixed[:, k * 128 : (k + 1) * 128], 64, 1) for k in range(2)]
    scores = mixed + jnp.concatenate(turned, axis=1) + jnp.concatenate([bias, bias], axis=1)
    top = jnp.max(scores, axis=0, keepdims=True)
    raised = jnp.exp(scores - top)
    attn = raised / jnp.sum(raised, axis=0, keepdims=True)
    back = jnp.where(lane2 < 64, exact_dot(from_group[0], attn), exact_dot(from_group[1], attn))
    upper = z >= ZS // 2
    obuf[:, 0, :] = jnp.where(upper, back[:, 128:], back[:, :128])
    obuf[:, 1, :] = jnp.where(upper, back[:, :128], back[:, 128:])
    pair = ylo * ZS + (z % (ZS // 2)) * 2 + core

    for off in (12, 3, 13, 2, 14, 1, 15):
        there = ((z + off) % ZS) * 2
        for side in (1 - ylo, ylo):
            for c in range(2):
                peer = side * 2 * ZS + there + c
                rdma(obuf.at[peer], abuf.at[pair], ssem.at[1], srsem.at[1], at(peer)).start()

    for peer in ((1 - ylo) * 2 * ZS + z * 2, (1 - ylo) * 2 * ZS + z * 2 + 1, partner):
        rdma(obuf.at[peer], abuf.at[pair], ssem.at[1], srsem.at[1], at(peer)).start()

    abuf[pair] = obuf[ci]
    await_bytes(abuf.at[pl.ds(0, 31)], srsem.at[1])
    low_sets, high_sets = abuf[:, 0, :], abuf[:, 1, :]
    received = jnp.concatenate([low_sets[0:16], high_sets[0:16], low_sets[16:32], high_sets[16:32]], axis=0)
    high, rest = split(received, 2)
    high, rest = high.astype(F32), rest.astype(F32)
    for q in range(8):
        lhs[q * 64 : (q + 1) * 64, 0:128] = jnp.where(lane // H == q, high, 0.0).astype(BF)
        lhs[q * 64 : (q + 1) * 64, 128:256] = jnp.where(lane // H == q, rest, 0.0).astype(BF)

    def weigh(j):
        spread = jnp.dot(lhs[...], expand[j], preferred_element_type=F32)
        return spread[:LOCS] * b[j, 0:LOCS, :].astype(F32) + spread[LOCS:] * b[j, LOCS:, :].astype(F32)

    @pl.loop(0, 4)
    def _(t):
        ps[t] = weigh((1 - core) * 4 + t).astype(BF)
        rdma(ps.at[t], pr.at[t], csem.at[0], crsem.at[t], at(partner)).start()

    @pl.loop(0, 4)
    def _(t):
        mixed_in = weigh(core * 4 + t)
        await_bytes(pr.at[t], crsem.at[t])
        own[t] = mixed_in + pr[t].astype(F32)
        theirs = pl.ds(pl.multiple_of((1 - ylo) * 128, 128), 128)
        ys[t] = own[t, theirs, :].astype(BF)
        rdma(ys.at[t], yr.at[t], csem.at[1], yrsem.at[t], at(ypartner)).start()

    def zdev(to):
        return at(ylo * 2 * ZS + to * 2 + core)

    def ahead(n):
        return (z + way * n + ZS) % ZS

    @pl.loop(0, 4)
    def _(t):
        mine = pl.ds(pl.multiple_of(ylo * 128, 128), 128)
        await_bytes(yr.at[t], yrsem.at[t])
        total = own[t, mine, :] + yr[t].astype(F32)
        total = total.reshape(ZS, 8, BLOCK)
        zf[t] = total
        zs[t] = total.astype(BF)
        for d in (8, 7, 6, 5):
            to, via = ahead(d), ahead(d - 4)
            rdma(zs.at[t, to], rin.at[t, 0, d - 5], zsem.at[0], rinsem.at[0, t], zdev(via)).start()
            if d < 8:
                to, via = ahead(-d), ahead(4 - d)
                rdma(zs.at[t, to], rin.at[t, 1, d - 5], zsem.at[0], rinsem.at[1, t], zdev(via)).start()
        for d in (3, 2, 1):
            for q, to in enumerate((ahead(d), ahead(-d))):
                rdma(zs.at[t, to], zr.at[t, q, d - 1], zsem.at[0], zrsem.at[t], zdev(to)).start()

    @pl.loop(0, 4)
    def _(t):
        for q, to, n in ((0, ahead(4), 4), (1, ahead(-4), 3)):
            await_bytes(rin.at[t, q, pl.ds(0, n)], rinsem.at[q, t])
            total = zf[t, to]
            for d in range(n):
                total = total + rin[t, q, d].astype(F32)
            rout[t, q] = total.astype(BF)
            rdma(rout.at[t, q], zr.at[t, q, 3], zsem.at[1], zrsem.at[t], zdev(to)).start()

    squares = jnp.zeros((8, 1), F32)
    for t in range(4):
        await_bytes(zr.at[t], zrsem.at[t])
        total = zf[t, z]
        for q in range(2):
            for d in range(4):
                total = total + zr[t, q, d].astype(F32)
        pooled[:, t * BLOCK : (t + 1) * BLOCK] = total
        squares = squares + jnp.sum(total * total, axis=1, keepdims=True)
    ssb[...] = jnp.broadcast_to(squares, (8, 128))
    share = rdma(ssb, ssr, csem.at[3], qrsem.at[0], at(partner))
    share.start()
    scaled = pooled[...] * gain[:, pl.ds(pl.multiple_of(core * 1024, 1024), 1024)]
    share.wait_recv()
    inverse = lax.rsqrt((squares + ssr[:, 0:1]) * (1.0 / E) + 1e-06)
    jt[core, ylo, z] = (scaled * inverse).astype(BF)

    def row_block(row, d):
        return jt.at[core, row, ahead(-d)]

    def spread(d, way_z, steps):
        for n in steps:
            block = row_block(ylo, d)
            there = (d + way_z * n) % ZS
            rdma(block, block, jsem.at[0], jz.at[there], zdev(ahead(way_z * n))).start()

    def share_block(d):
        block = row_block(ylo, d)
        rdma(block, block, jsem.at[1], jy.at[d], at(ypartner)).start()
        rdma(block, block, jsem.at[2], jc.at[d], at(partner)).start()

    for n in (4, 3, 2, 1):
        spread(0, 1, (n,))
        spread(0, -1, (n,))
    share_block(0)
    order = (4, 12, 1, 15, 2, 14, 3, 13, 5, 11, 6, 10, 7, 9, 8)
    for d in order:
        await_bytes(row_block(ylo, d), jz.at[d])
        if d == 4:
            spread(4, 1, (4, 3, 2, 1))
        if d == 12:
            spread(12, -1, (3, 2, 1))
        share_block(d)
    def decode_own(row):
        side = jt[core, row].reshape(128, 1024)

        @pl.loop(0, BUNDLE, unroll=True)
        def _(c):
            part = wd[c, pl.ds(pl.multiple_of(core * 1024, 1024), 1024), :]
            dec[c] = jnp.dot(side, part, preferred_element_type=F32) + hbias[pl.ds(c, 1), :]

    def decode_rest(row):
        side = jt[1 - core, row].reshape(128, 1024)

        @pl.loop(0, BUNDLE, unroll=True)
        def _(c):
            part = wd[c, pl.ds(pl.multiple_of((1 - core) * 1024, 1024), 1024), :]
            rows = pl.ds(pl.multiple_of(row * 128, 128), 128)
            columns = pl.ds(pl.multiple_of(c * BLOCK, BLOCK), BLOCK)
            out[rows, columns] = (dec[c] + jnp.dot(side, part, preferred_element_type=F32)).astype(BF)

    decode_own(ylo)
    for d in range(ZS):
        await_bytes(jt.at[1 - core, ylo, ahead(d)], jc.at[d])
    decode_rest(ylo)
    for d in (0, *order):
        block = row_block(1 - ylo, d)
        await_bytes(block, jy.at[d])
        rdma(block, block, jsem.at[2], jd.at[d], at(partner)).start()
    decode_own(1 - ylo)
    for d in range(ZS):
        await_bytes(jt.at[1 - core, 1 - ylo, ahead(d)], jd.at[d])
    decode_rest(1 - ylo)

    await_bytes(wg.at[pl.ds(0, 7)], esem.at[0])
    await_bytes(sbuf.at[pl.ds(0, CHAN - 1)], ssem.at[0])
    await_bytes(obuf.at[pl.ds(0, 31)], ssem.at[1])
    await_bytes(ps, csem.at[0])
    await_bytes(ys, csem.at[1])
    await_bytes(zs.at[:, pl.ds(0, 13)], zsem.at[0])
    await_bytes(rout, zsem.at[1])
    share.wait_send()
    await_bytes(jt.at[0, 0, pl.ds(0, ZS - 1)], jsem.at[0])
    await_bytes(jt.at[0, 0], jsem.at[1])
    await_bytes(jt.at[0], jsem.at[2])


def shards(
    pixels,
    patch_mask,
    group_map,
    embed_weight,
    mask_token,
    chan_embed,
    agg_weight,
    query_key,
    group_bias,
    norm_gain,
    head_weight,
    head_bias,
):
    vmem = pl.BlockSpec(memory_space=pltpu.VMEM)
    hbm = pl.BlockSpec(memory_space=pltpu.HBM)
    dma = pltpu.SemaphoreType.DMA
    decoded = pl.pallas_call(
        kernel,
        out_shape=jax.ShapeDtypeStruct((LOCS, BUNDLE * BLOCK), BF),
        in_specs=[hbm] * 13,
        out_specs=vmem,
        scratch_shapes=[
            pltpu.VMEM((LOCS, BUNDLE, BLOCK), BF),
            pltpu.VMEM((BUNDLE, LOCS), jnp.int32),
            pltpu.VMEM((16, 128), BF),
            pltpu.VMEM((BUNDLE, E), BF),
            pltpu.SMEM((BUNDLE,), F32),
            pltpu.SMEM((C,), jnp.int32),
            pltpu.VMEM((1, C), jnp.int32),
            pltpu.VMEM((H, E), BF),
            pltpu.VMEM((H, G), F32),
            pltpu.VMEM((1, E), F32),
            pltpu.VMEM((E, BUNDLE, BLOCK), BF),
            pltpu.VMEM((BUNDLE, BLOCK), F32),
            pltpu.VMEM((16, 128), F32),
            pltpu.VMEM((BUNDLE, LOCS, 128), F32),
            pltpu.VMEM((BUNDLE * LOCS, BLOCK + 128), BF),
            pltpu.VMEM((BUNDLE, E, BLOCK), BF),
            pltpu.VMEM((BUNDLE, 128, BLOCK), F32),
            pltpu.VMEM((8, 2, 128, BLOCK), BF),
            pltpu.VMEM((8, 2 * LOCS, BLOCK), BF),
            pltpu.VMEM((BUNDLE * LOCS, BLOCK), F32),
            pltpu.VMEM((2 * LOCS, 128), F32),
            pltpu.VMEM((8, BLOCK, BLOCK), BF),
            pltpu.VMEM((CHAN, 2, 128), F32),
            pltpu.VMEM((CHAN, 2, 128), F32),
            pltpu.VMEM((CHAN, 2, 128), F32),
            pltpu.VMEM((CHAN // 2, 2, 128), F32),
            pltpu.VMEM((2 * LOCS, 256), BF),
            pltpu.VMEM((4, LOCS, BLOCK), BF),
            pltpu.VMEM((4, LOCS, BLOCK), BF),
            pltpu.VMEM((4, LOCS, BLOCK), F32),
            pltpu.VMEM((4, 128, BLOCK), BF),
            pltpu.VMEM((4, 128, BLOCK), BF),
            pltpu.VMEM((4, ZS, 8, BLOCK), BF),
            pltpu.VMEM((4, ZS, 8, BLOCK), F32),
            pltpu.VMEM((4, 2, 4, 8, BLOCK), BF),
            pltpu.VMEM((4, 2, 4, 8, BLOCK), BF),
            pltpu.VMEM((4, 2, 8, BLOCK), BF),
            pltpu.VMEM((8, 1024), F32),
            pltpu.VMEM((8, 128), F32),
            pltpu.VMEM((8, 128), F32),
            pltpu.VMEM((2, 2, ZS, 8, 1024), BF),
            dma((14,)),
            dma((1,)),
            dma((8,)),
            dma((8,)),
            dma((2,)),
            dma((2,)),
            dma((4,)),
            dma((4,)),
            dma((4,)),
            dma((2,)),
            dma((2, 4)),
            dma((4,)),
            dma((1,)),
            dma((3,)),
            dma((ZS,)),
            dma((ZS,)),
            dma((ZS,)),
            dma((ZS,)),
        ],
        compiler_params=pltpu.CompilerParams(
            collective_id=0, has_side_effects=True, vmem_limit_bytes=32 * 1024 * 1024
        ),
    )(*[pltpu.with_memory_space_constraint(v, pltpu.HBM) for v in (
        pixels,
        patch_mask.T,
        embed_weight,
        mask_token.reshape(16, 128),
        chan_embed,
        agg_weight,
        group_map,
        group_map.reshape(1, C),
        query_key,
        group_bias,
        norm_gain.reshape(1, E),
        head_weight,
        head_bias,
    )])
    return decoded.reshape(pixels.shape)


def solution(mesh):
    return jax.shard_map(
        shards,
        mesh=mesh,
        in_specs=(
            P("loc", "chan", None),
            P("loc", "chan"),
            P(),
            P(None, "loc"),
            P(),
            P("chan", None),
            P("chan"),
            P(),
            P(),
            P(),
            P(None, "chan", None),
            P("chan", None),
        ),
        out_specs=P("loc", "chan", None),
        check_vma=False,
    )
```

```python
import functools
import math

import jax
import jax.numpy as jnp
from jax import lax
from jax.experimental import pallas as pl
from jax.experimental.pallas import tpu as pltpu
from jax.sharding import PartitionSpec as P

C = 256
E = 2048
G = 64
H = 16
BUNDLE = 4
LOCS = 256
CHAN = 64
ZS = 16
BLOCK = 256
BF = jnp.bfloat16
F32 = jnp.float32
MESH = pl.DeviceIdType.MESH


def split(value, parts):
    pieces = []
    for _ in range(parts - 1):
        piece = value.astype(BF)
        pieces.append(piece)
        value = value - piece.astype(F32)
    return [*pieces, value.astype(BF)]


def exact_dot(onehot, value):
    return sum(jnp.dot(onehot, piece, preferred_element_type=F32) for piece in split(value, 3))


def kernel(
    pixels_h,
    mask_h,
    emb_h,
    token_h,
    ce_h,
    agg_h,
    map_h,
    gmv_h,
    qk_h,
    gbias_h,
    gain_h,
    head_h,
    hbias_h,
    out,
    raw,
    maskv,
    token,
    ce,
    agg,
    gm_s,
    gm_v,
    qk,
    gbias,
    gain,
    hraw,
    hbias,
    tokf,
    keep,
    px,
    wd,
    dec,
    wg,
    b,
    pre,
    acc,
    expand,
    sbuf,
    rbuf,
    obuf,
    abuf,
    lhs,
    ps,
    pr,
    own,
    ys,
    yr,
    zs,
    zf,
    zr,
    rin,
    rout,
    pooled,
    ssb,
    ssr,
    jt,
    lsem,
    esem,
    rsem,
    psem,
    ssem,
    srsem,
    csem,
    crsem,
    yrsem,
    zsem,
    rinsem,
    zrsem,
    qrsem,
    jsem,
    jz,
    jy,
    jc,
    jd,
):
    ci = lax.axis_index("chan")
    li = lax.axis_index("loc")
    core = ci % 2
    z = (ci // 2) % ZS
    ylo = ci // (2 * ZS)
    x = li % 4
    yhi = li // 4
    way = 1 - 2 * core
    partner = ci + way
    ypartner = (ci + 2 * ZS) % CHAN
    nxt = yhi * 4 + (x + way + 4) % 4
    prv = yhi * 4 + (x - way + 4) % 4
    cross_loc = (1 - yhi) * 4 + x

    def at(chan, loc=None):
        return {"chan": chan, "loc": li if loc is None else loc}

    def rdma(src, dst, send, recv, where):
        return pltpu.make_async_remote_copy(
            src_ref=src, dst_ref=dst, send_sem=send, recv_sem=recv, device_id=where, device_id_type=MESH
        )

    def await_bytes(ref, sem):
        pltpu.make_async_copy(ref, ref, sem).wait()

    diagonals = [(1 - yhi) * 4 + n % 4 for n in (nxt, prv)]

    def load(k, src, dst):
        copy = pltpu.make_async_copy(src, dst, lsem.at[k])
        copy.start()
        return copy

    first_half = load(0, emb_h.at[pl.ds(0, 128)], wg.at[li, 0])
    other_half = load(1, emb_h.at[pl.ds(128, 128)], wg.at[li, 1])

    def for_peers(act):
        @pl.loop(0, ZS - 1)
        def _(e):
            off = 8 - (e % 2) * ((e + 1) // 2) + (1 - e % 2) * (e // 2)
            there = ((z + off) % ZS) * 2
            for side in (1 - ylo, ylo):
                for c in range(2):
                    act(side * 2 * ZS + there + c)

        act((1 - ylo) * 2 * ZS + z * 2)
        act((1 - ylo) * 2 * ZS + z * 2 + 1)
        act(partner)

    barrier = pltpu.get_barrier_semaphore()
    for chan, loc in ((ci, nxt), (ci, prv), (ypartner, cross_loc), *((ypartner, d) for d in diagonals)):
        pl.semaphore_signal(barrier, inc=1, device_id=at(chan, loc), device_id_type=MESH)
    for_peers(lambda p: pl.semaphore_signal(barrier, inc=1, device_id=at(p), device_id_type=MESH))
    loads = [
        load(2, pixels_h, raw),
        load(3, mask_h, maskv),
        load(4, token_h, token),
        load(5, ce_h, ce),
        load(6, agg_h, agg),
        load(7, map_h, gm_s),
        load(8, gmv_h, gm_v),
        load(9, qk_h, qk),
        load(10, gbias_h, gbias),
        load(11, gain_h, gain),
        load(12, hbias_h, hbias),
    ]
    heads = load(13, head_h, hraw)

    def place(t, row):
        return ((yhi + row) % 2) * 4 + (x + way * ((3 * t * t - 5 * t) // 2) + 8) % 4

    swapped = {1: 1, 2: 4, 3: 5, 4: 2, 5: 3, 6: 6, 7: 7}

    def half(step):
        return wg.at[place(step // 2, step % 2), core]

    def pass_on(step, to, loc):
        rdma(half(step), half(step), esem.at[0], rsem.at[to], at(ci, loc)).start()

    def to_partner(step):
        rdma(half(step), half(step), esem.at[0], psem.at[swapped[step]], at(partner)).start()

    def arrived(step):
        await_bytes(half(step), rsem.at[step])

    first_half.wait()
    other_half.wait()
    for copy in loads:
        copy.wait()

    base = ci * BUNDLE
    groups = [gm_s[base + k] for k in range(BUNDLE)]
    low = jnp.minimum(jnp.minimum(groups[0], groups[1]), jnp.minimum(groups[2], groups[3]))
    weights = []
    for k in range(BUNDLE):
        full = 0.5 * agg[k]
        second = jnp.where(groups[k] != low, full, 0.0)
        weights.append((full - second, second))

    acc[...] = jnp.zeros_like(acc)
    tokf[...] = token[...].astype(F32)

    @pl.loop(0, BUNDLE)
    def _(c):
        hid = jnp.broadcast_to(maskv[pl.ds(c, 1), :].astype(F32), (128, LOCS)).T
        rows = pl.ds(pl.multiple_of(c * LOCS, LOCS), LOCS)
        at_lane = lax.broadcasted_iota(jnp.int32, (LOCS, 128), 1)
        px[rows, BLOCK:] = jnp.where(at_lane == 0, hid, jnp.where(at_lane == 1 + c, 1.0, 0.0)).astype(BF)
        keep[c] = 1.0 - hid

    @pl.loop(0, LOCS // 32)
    def _(i):
        rows = pl.ds(pl.multiple_of(i * 32, 32), 32)
        turned = jnp.swapaxes(raw[rows], 0, 1)
        for c in range(BUNDLE):
            shown = keep[c, rows, :]
            kept = turned[c].astype(F32) * jnp.concatenate([shown, shown], axis=1)
            px[pl.ds(pl.multiple_of(c * LOCS + i * 32, 32), 32), 0:BLOCK] = kept.astype(BF)

    @pl.loop(0, 8)
    def _(step):
        p = lax.broadcasted_iota(jnp.int32, (BLOCK, BLOCK), 0) % H
        head = 2 * step + lax.broadcasted_iota(jnp.int32, (BLOCK, BLOCK), 1) // 128
        expand[step] = jnp.where(p == head, 1.0, 0.0).astype(BF)

    row16 = lax.broadcasted_iota(jnp.int32, (128, BLOCK), 0)

    def embed_block(j):
        columns = pl.ds(pl.multiple_of(j * BLOCK, BLOCK), BLOCK)
        hide = jnp.concatenate([tokf[pl.ds(2 * j, 1), :], tokf[pl.ds(2 * j + 1, 1), :]], axis=1)
        extra = jnp.where(row16 == 0, hide, 0.0)
        embeds = ce[:, columns].astype(F32)
        for k in range(BUNDLE):
            extra = jnp.where(row16 == 1 + k, embeds[k : k + 1], extra)
        weight = jnp.concatenate([wg[j].reshape(BLOCK, BLOCK), extra.astype(BF)], axis=0)
        pre[...] = jnp.dot(px[...], weight, preferred_element_type=F32)

        @pl.loop(0, LOCS // 32, unroll=True)
        def _(chunk):
            first, second = None, None
            for k in range(BUNDLE):
                v = pre[pl.ds(pl.multiple_of(k * LOCS + chunk * 32, 32), 32), :]
                g = v + v * lax.erf(v * (1.0 / math.sqrt(2.0)))
                w0, w1 = weights[k]
                first = g * w0 if first is None else first + g * w0
                second = g * w1 if second is None else second + g * w1
            b[j, pl.ds(pl.multiple_of(chunk * 32, 32), 32), :] = first.astype(BF)
            b[j, pl.ds(pl.multiple_of(LOCS + chunk * 32, 32), 32), :] = second.astype(BF)

        q = jnp.concatenate([qk[:, columns]] * 8, axis=0)
        acc[...] += lax.dot_general(b[j], q, (((1,), (1,)), ((), ())), preferred_element_type=F32)

    embed_block(li)
    pl.semaphore_wait(barrier, CHAN - 1 + 5)
    mine = wg.at[li, core]
    rdma(mine, mine, esem.at[0], rsem.at[2], at(ci, nxt)).start()
    rdma(mine, mine, esem.at[0], rsem.at[4], at(ci, prv)).start()
    rdma(mine, mine, esem.at[0], rsem.at[1], at(ypartner, cross_loc)).start()
    rdma(mine, mine, esem.at[0], rsem.at[3], at(ypartner, diagonals[0])).start()

    @pl.loop(1, 8)
    def _(step):
        @pl.when(step == 1)
        def _():
            arrived(2)
            pass_on(2, 6, nxt)
            to_partner(2)
            arrived(4)
            to_partner(4)
            rdma(mine, mine, esem.at[0], rsem.at[5], at(ypartner, diagonals[1])).start()

        @pl.when(step == 2)
        def _():
            arrived(1)
            to_partner(1)

        @pl.when(step == 3)
        def _():
            arrived(3)
            pass_on(3, 7, nxt)
            to_partner(3)
            arrived(6)
            to_partner(6)

        @pl.when(step == 4)
        def _():
            arrived(5)
            to_partner(5)

        @pl.when(step == 6)
        def _():
            arrived(7)
            to_partner(7)

        third = ((step // 3) % 2) * (1 - (step % 3 + 1) // 2)
        fourth = (step // 4) * (1 - (step % 4 + 3) // 4)
        turn = step + third - fourth
        t, row = turn % 4, turn // 4
        j = place(t, row)
        await_bytes(wg.at[j, 1 - core], psem.at[2 * t + row])
        embed_block(j)

    lane = lax.broadcasted_iota(jnp.int32, (CHAN, 128), 1)
    part = jnp.zeros((CHAN, 128), F32)
    for q in range(8):
        part = part + jnp.where(lane // H == q, acc[q * 64 : (q + 1) * 64, :], 0.0)
    sbuf[:, 0, :] = part
    sbuf[:, 1, :] = jnp.concatenate([part[16:32], part[0:16], part[48:64], part[32:48]], axis=0)

    for_peers(lambda p: rdma(sbuf.at[p], rbuf.at[ci], ssem.at[0], srsem.at[0], at(p)).start())

    rbuf[ci] = sbuf[ci]
    gmap = jnp.broadcast_to(gm_v[...].astype(F32), (8, C))
    wide = lax.broadcasted_iota(jnp.int32, (CHAN, C), 1)
    bund = lax.broadcasted_iota(jnp.int32, (CHAN, C), 0)
    inside = wide // BUNDLE == bund
    lows = jnp.min(jnp.where(inside, gmap[0:1], 1e9), axis=1, keepdims=True)
    highs = jnp.max(jnp.where(inside, gmap[0:1], -1.0), axis=1, keepdims=True)
    gcol = lax.broadcasted_iota(jnp.int32, (CHAN, G), 1).astype(F32)
    from_group = [jnp.where(v == gcol, 1.0, 0.0).astype(BF) for v in (lows, highs)]
    to_group = [f.astype(F32).T.astype(BF) for f in from_group]

    bias = jnp.concatenate([gbias[...]] * 8, axis=0).T
    heads.wait()

    @pl.loop(0, E // 32)
    def _(i):
        rows = pl.ds(pl.multiple_of(i * 32, 32), 32)
        wd[:, rows, :] = jnp.swapaxes(hraw[rows], 0, 1)

    await_bytes(rbuf.at[pl.ds(0, CHAN - 1)], srsem.at[0])
    lane2 = lax.broadcasted_iota(jnp.int32, (CHAN, 256), 1) % 128
    got = jnp.concatenate([rbuf[:, 0, :], rbuf[:, 1, :]], axis=1)
    mixed = jnp.where(lane2 < 64, exact_dot(to_group[0], got), exact_dot(to_group[1], got))
    turned = [pltpu.roll(mixed[:, k * 128 : (k + 1) * 128], 64, 1) for k in range(2)]
    scores = mixed + jnp.concatenate(turned, axis=1) + jnp.concatenate([bias, bias], axis=1)
    top = jnp.max(scores, axis=0, keepdims=True)
    raised = jnp.exp(scores - top)
    attn = raised / jnp.sum(raised, axis=0, keepdims=True)
    back = jnp.where(lane2 < 64, exact_dot(from_group[0], attn), exact_dot(from_group[1], attn))
    upper = z >= ZS // 2
    obuf[:, 0, :] = jnp.where(upper, back[:, 128:], back[:, :128])
    obuf[:, 1, :] = jnp.where(upper, back[:, :128], back[:, 128:])
    pair = ylo * ZS + (z % (ZS // 2)) * 2 + core

    for off in (12, 3, 13, 2, 14, 1, 15):
        there = ((z + off) % ZS) * 2
        for side in (1 - ylo, ylo):
            for c in range(2):
                peer = side * 2 * ZS + there + c
                rdma(obuf.at[peer], abuf.at[pair], ssem.at[1], srsem.at[1], at(peer)).start()

    for peer in ((1 - ylo) * 2 * ZS + z * 2, (1 - ylo) * 2 * ZS + z * 2 + 1, partner):
        rdma(obuf.at[peer], abuf.at[pair], ssem.at[1], srsem.at[1], at(peer)).start()

    abuf[pair] = obuf[ci]
    await_bytes(abuf.at[pl.ds(0, 31)], srsem.at[1])
    low_sets, high_sets = abuf[:, 0, :], abuf[:, 1, :]
    received = jnp.concatenate([low_sets[0:16], high_sets[0:16], low_sets[16:32], high_sets[16:32]], axis=0)
    high, rest = split(received, 2)
    high, rest = high.astype(F32), rest.astype(F32)
    for q in range(8):
        lhs[q * 64 : (q + 1) * 64, 0:128] = jnp.where(lane // H == q, high, 0.0).astype(BF)
        lhs[q * 64 : (q + 1) * 64, 128:256] = jnp.where(lane // H == q, rest, 0.0).astype(BF)

    def weigh(j):
        spread = jnp.dot(lhs[...], expand[j], preferred_element_type=F32)
        return spread[:LOCS] * b[j, 0:LOCS, :].astype(F32) + spread[LOCS:] * b[j, LOCS:, :].astype(F32)

    @pl.loop(0, 4, unroll=True)
    def _(t):
        ps[t] = weigh((1 - core) * 4 + t).astype(BF)
        rdma(ps.at[t], pr.at[t], csem.at[0], crsem.at[t], at(partner)).start()

    @pl.loop(0, 4, unroll=True)
    def _(t):
        mixed_in = weigh(core * 4 + t)
        await_bytes(pr.at[t], crsem.at[t])
        own[t] = mixed_in + pr[t].astype(F32)
        theirs = pl.ds(pl.multiple_of((1 - ylo) * 128, 128), 128)
        ys[t] = own[t, theirs, :].astype(BF)
        rdma(ys.at[t], yr.at[t], csem.at[1], yrsem.at[t], at(ypartner)).start()

    def zdev(to):
        return at(ylo * 2 * ZS + to * 2 + core)

    def ahead(n):
        return (z + way * n + ZS) % ZS

    @pl.loop(0, 4, unroll=True)
    def _(t):
        mine = pl.ds(pl.multiple_of(ylo * 128, 128), 128)
        await_bytes(yr.at[t], yrsem.at[t])
        total = own[t, mine, :] + yr[t].astype(F32)
        total = total.reshape(ZS, 8, BLOCK)
        zf[t] = total
        zs[t] = total.astype(BF)
        for d in (8, 7, 6, 5):
            to, via = ahead(d), ahead(d - 4)
            rdma(zs.at[t, to], rin.at[t, 0, d - 5], zsem.at[0], rinsem.at[0, t], zdev(via)).start()
            if d < 8:
                to, via = ahead(-d), ahead(4 - d)
                rdma(zs.at[t, to], rin.at[t, 1, d - 5], zsem.at[0], rinsem.at[1, t], zdev(via)).start()
        for d in (3, 2, 1):
            for q, to in enumerate((ahead(d), ahead(-d))):
                rdma(zs.at[t, to], zr.at[t, q, d - 1], zsem.at[0], zrsem.at[t], zdev(to)).start()

    @pl.loop(0, 4, unroll=True)
    def _(t):
        for q, to, n in ((0, ahead(4), 4), (1, ahead(-4), 3)):
            await_bytes(rin.at[t, q, pl.ds(0, n)], rinsem.at[q, t])
            total = zf[t, to]
            for d in range(n):
                total = total + rin[t, q, d].astype(F32)
            rout[t, q] = total.astype(BF)
            rdma(rout.at[t, q], zr.at[t, q, 3], zsem.at[1], zrsem.at[t], zdev(to)).start()

    squares = jnp.zeros((8, 1), F32)
    for t in range(4):
        await_bytes(zr.at[t], zrsem.at[t])
        total = zf[t, z]
        for q in range(2):
            for d in range(4):
                total = total + zr[t, q, d].astype(F32)
        pooled[:, t * BLOCK : (t + 1) * BLOCK] = total
        squares = squares + jnp.sum(total * total, axis=1, keepdims=True)
    ssb[...] = jnp.broadcast_to(squares, (8, 128))
    share = rdma(ssb, ssr, csem.at[3], qrsem.at[0], at(partner))
    share.start()
    scaled = pooled[...] * gain[:, pl.ds(pl.multiple_of(core * 1024, 1024), 1024)]
    share.wait_recv()
    inverse = lax.rsqrt((squares + ssr[:, 0:1]) * (1.0 / E) + 1e-06)
    jt[core, ylo, z] = (scaled * inverse).astype(BF)

    def row_block(row, d):
        return jt.at[core, row, ahead(-d)]

    def spread(d, way_z, steps):
        for n in steps:
            block = row_block(ylo, d)
            there = (d + way_z * n) % ZS
            rdma(block, block, jsem.at[0], jz.at[there], zdev(ahead(way_z * n))).start()

    def share_block(d):
        block = row_block(ylo, d)
        rdma(block, block, jsem.at[1], jy.at[d], at(ypartner)).start()
        rdma(block, block, jsem.at[2], jc.at[d], at(partner)).start()

    for n in (4, 3, 2, 1):
        spread(0, 1, (n,))
        spread(0, -1, (n,))
    share_block(0)
    order = (4, 12, 1, 15, 2, 14, 3, 13, 5, 11, 6, 10, 7, 9, 8)
    for d in order:
        await_bytes(row_block(ylo, d), jz.at[d])
        if d == 4:
            spread(4, 1, (4, 3, 2, 1))
        if d == 12:
            spread(12, -1, (3, 2, 1))
        share_block(d)
    def decode_own(row):
        side = jt[core, row].reshape(128, 1024)

        @pl.loop(0, BUNDLE, unroll=True)
        def _(c):
            part = wd[c, pl.ds(pl.multiple_of(core * 1024, 1024), 1024), :]
            dec[c] = jnp.dot(side, part, preferred_element_type=F32) + hbias[pl.ds(c, 1), :]

    def decode_rest(row):
        side = jt[1 - core, row].reshape(128, 1024)

        @pl.loop(0, BUNDLE, unroll=True)
        def _(c):
            part = wd[c, pl.ds(pl.multiple_of((1 - core) * 1024, 1024), 1024), :]
            rows = pl.ds(pl.multiple_of(row * 128, 128), 128)
            columns = pl.ds(pl.multiple_of(c * BLOCK, BLOCK), BLOCK)
            out[rows, columns] = (dec[c] + jnp.dot(side, part, preferred_element_type=F32)).astype(BF)

    decode_own(ylo)
    for d in range(ZS):
        await_bytes(jt.at[1 - core, ylo, ahead(d)], jc.at[d])
    decode_rest(ylo)
    for d in (0, *order):
        block = row_block(1 - ylo, d)
        await_bytes(block, jy.at[d])
        rdma(block, block, jsem.at[2], jd.at[d], at(partner)).start()
    decode_own(1 - ylo)
    for d in range(ZS):
        await_bytes(jt.at[1 - core, 1 - ylo, ahead(d)], jd.at[d])
    decode_rest(1 - ylo)

    await_bytes(wg.at[pl.ds(0, 7)], esem.at[0])
    await_bytes(sbuf.at[pl.ds(0, CHAN - 1)], ssem.at[0])
    await_bytes(obuf.at[pl.ds(0, 31)], ssem.at[1])
    await_bytes(ps, csem.at[0])
    await_bytes(ys, csem.at[1])
    await_bytes(zs.at[:, pl.ds(0, 13)], zsem.at[0])
    await_bytes(rout, zsem.at[1])
    share.wait_send()
    await_bytes(jt.at[0, 0, pl.ds(0, ZS - 1)], jsem.at[0])
    await_bytes(jt.at[0, 0], jsem.at[1])
    await_bytes(jt.at[0], jsem.at[2])


def shards(
    pixels,
    patch_mask,
    group_map,
    embed_weight,
    mask_token,
    chan_embed,
    agg_weight,
    query_key,
    group_bias,
    norm_gain,
    head_weight,
    head_bias,
):
    vmem = pl.BlockSpec(memory_space=pltpu.VMEM)
    hbm = pl.BlockSpec(memory_space=pltpu.HBM)
    dma = pltpu.SemaphoreType.DMA
    decoded = pl.pallas_call(
        kernel,
        out_shape=jax.ShapeDtypeStruct((LOCS, BUNDLE * BLOCK), BF),
        in_specs=[hbm] * 13,
        out_specs=vmem,
        scratch_shapes=[
            pltpu.VMEM((LOCS, BUNDLE, BLOCK), BF),
            pltpu.VMEM((BUNDLE, LOCS), jnp.int32),
            pltpu.VMEM((16, 128), BF),
            pltpu.VMEM((BUNDLE, E), BF),
            pltpu.SMEM((BUNDLE,), F32),
            pltpu.SMEM((C,), jnp.int32),
            pltpu.VMEM((1, C), jnp.int32),
            pltpu.VMEM((H, E), BF),
            pltpu.VMEM((H, G), F32),
            pltpu.VMEM((1, E), F32),
            pltpu.VMEM((E, BUNDLE, BLOCK), BF),
            pltpu.VMEM((BUNDLE, BLOCK), F32),
            pltpu.VMEM((16, 128), F32),
            pltpu.VMEM((BUNDLE, LOCS, 128), F32),
            pltpu.VMEM((BUNDLE * LOCS, BLOCK + 128), BF),
            pltpu.VMEM((BUNDLE, E, BLOCK), BF),
            pltpu.VMEM((BUNDLE, 128, BLOCK), F32),
            pltpu.VMEM((8, 2, 128, BLOCK), BF),
            pltpu.VMEM((8, 2 * LOCS, BLOCK), BF),
            pltpu.VMEM((BUNDLE * LOCS, BLOCK), F32),
            pltpu.VMEM((2 * LOCS, 128), F32),
            pltpu.VMEM((8, BLOCK, BLOCK), BF),
            pltpu.VMEM((CHAN, 2, 128), F32),
            pltpu.VMEM((CHAN, 2, 128), F32),
            pltpu.VMEM((CHAN, 2, 128), F32),
            pltpu.VMEM((CHAN // 2, 2, 128), F32),
            pltpu.VMEM((2 * LOCS, 256), BF),
            pltpu.VMEM((4, LOCS, BLOCK), BF),
            pltpu.VMEM((4, LOCS, BLOCK), BF),
            pltpu.VMEM((4, LOCS, BLOCK), F32),
            pltpu.VMEM((4, 128, BLOCK), BF),
            pltpu.VMEM((4, 128, BLOCK), BF),
            pltpu.VMEM((4, ZS, 8, BLOCK), BF),
            pltpu.VMEM((4, ZS, 8, BLOCK), F32),
            pltpu.VMEM((4, 2, 4, 8, BLOCK), BF),
            pltpu.VMEM((4, 2, 4, 8, BLOCK), BF),
            pltpu.VMEM((4, 2, 8, BLOCK), BF),
            pltpu.VMEM((8, 1024), F32),
            pltpu.VMEM((8, 128), F32),
            pltpu.VMEM((8, 128), F32),
            pltpu.VMEM((2, 2, ZS, 8, 1024), BF),
            dma((14,)),
            dma((1,)),
            dma((8,)),
            dma((8,)),
            dma((2,)),
            dma((2,)),
            dma((4,)),
            dma((4,)),
            dma((4,)),
            dma((2,)),
            dma((2, 4)),
            dma((4,)),
            dma((1,)),
            dma((3,)),
            dma((ZS,)),
            dma((ZS,)),
            dma((ZS,)),
            dma((ZS,)),
        ],
        compiler_params=pltpu.CompilerParams(
            collective_id=0, has_side_effects=True, vmem_limit_bytes=32 * 1024 * 1024
        ),
    )(*[pltpu.with_memory_space_constraint(v, pltpu.HBM) for v in (
        pixels,
        patch_mask.T,
        embed_weight,
        mask_token.reshape(16, 128),
        chan_embed,
        agg_weight,
        group_map,
        group_map.reshape(1, C),
        query_key,
        group_bias,
        norm_gain.reshape(1, E),
        head_weight,
        head_bias,
    )])
    return decoded.reshape(pixels.shape)


def solution(mesh):
    return jax.shard_map(
        shards,
        mesh=mesh,
        in_specs=(
            P("loc", "chan", None),
            P("loc", "chan"),
            P(),
            P(None, "loc"),
            P(),
            P("chan", None),
            P("chan"),
            P(),
            P(),
            P(),
            P(None, "chan", None),
            P("chan", None),
        ),
        out_specs=P("loc", "chan", None),
        check_vma=False,
    )
```

```python
import functools
import math

import jax
import jax.numpy as jnp
from jax import lax
from jax.experimental import pallas as pl
from jax.experimental.pallas import tpu as pltpu
from jax.sharding import PartitionSpec as P

C = 256
E = 2048
G = 64
H = 16
BUNDLE = 4
LOCS = 256
CHAN = 64
ZS = 16
BLOCK = 256
BF = jnp.bfloat16
F32 = jnp.float32
MESH = pl.DeviceIdType.MESH


def split(value, parts):
    pieces = []
    for _ in range(parts - 1):
        piece = value.astype(BF)
        pieces.append(piece)
        value = value - piece.astype(F32)
    return [*pieces, value.astype(BF)]


def exact_dot(onehot, value):
    return sum(jnp.dot(onehot, piece, preferred_element_type=F32) for piece in split(value, 3))


def kernel(
    pixels_h,
    mask_h,
    emb_h,
    token_h,
    ce_h,
    agg_h,
    map_h,
    gmv_h,
    qk_h,
    gbias_h,
    gain_h,
    head_h,
    hbias_h,
    out,
    raw,
    maskv,
    token,
    ce,
    agg,
    gm_s,
    gm_v,
    qk,
    gbias,
    gain,
    hraw,
    hbias,
    tokf,
    keep,
    px,
    wd,
    dec,
    wg,
    b,
    pre,
    acc,
    expand,
    sbuf,
    rbuf,
    obuf,
    abuf,
    lhs,
    ps,
    pr,
    own,
    ys,
    yr,
    zs,
    zf,
    zr,
    rin,
    rout,
    pooled,
    ssb,
    ssr,
    jt,
    lsem,
    esem,
    rsem,
    psem,
    ssem,
    srsem,
    csem,
    crsem,
    yrsem,
    zsem,
    rinsem,
    zrsem,
    qrsem,
    jsem,
    jz,
    jy,
    jc,
    jd,
):
    ci = lax.axis_index("chan")
    li = lax.axis_index("loc")
    core = ci % 2
    z = (ci // 2) % ZS
    ylo = ci // (2 * ZS)
    x = li % 4
    yhi = li // 4
    way = 1 - 2 * core
    partner = ci + way
    ypartner = (ci + 2 * ZS) % CHAN
    nxt = yhi * 4 + (x + way + 4) % 4
    prv = yhi * 4 + (x - way + 4) % 4
    cross_loc = (1 - yhi) * 4 + x

    def at(chan, loc=None):
        return {"chan": chan, "loc": li if loc is None else loc}

    def rdma(src, dst, send, recv, where):
        return pltpu.make_async_remote_copy(
            src_ref=src, dst_ref=dst, send_sem=send, recv_sem=recv, device_id=where, device_id_type=MESH
        )

    def await_bytes(ref, sem):
        pltpu.make_async_copy(ref, ref, sem).wait()

    diagonals = [(1 - yhi) * 4 + n % 4 for n in (nxt, prv)]

    def load(k, src, dst):
        copy = pltpu.make_async_copy(src, dst, lsem.at[k])
        copy.start()
        return copy

    first_half = load(0, emb_h.at[pl.ds(0, 128)], wg.at[li, 0])
    other_half = load(1, emb_h.at[pl.ds(128, 128)], wg.at[li, 1])

    def for_peers(act):
        @pl.loop(0, ZS - 1)
        def _(e):
            off = 8 - (e % 2) * ((e + 1) // 2) + (1 - e % 2) * (e // 2)
            there = ((z + off) % ZS) * 2
            for side in (1 - ylo, ylo):
                for c in range(2):
                    act(side * 2 * ZS + there + c)

        act((1 - ylo) * 2 * ZS + z * 2)
        act((1 - ylo) * 2 * ZS + z * 2 + 1)
        act(partner)

    barrier = pltpu.get_barrier_semaphore()
    for chan, loc in ((ci, nxt), (ci, prv), (ypartner, cross_loc), *((ypartner, d) for d in diagonals)):
        pl.semaphore_signal(barrier, inc=1, device_id=at(chan, loc), device_id_type=MESH)
    for_peers(lambda p: pl.semaphore_signal(barrier, inc=1, device_id=at(p), device_id_type=MESH))
    loads = [
        load(2, pixels_h, raw),
        load(3, mask_h, maskv),
        load(4, token_h, token),
        load(5, ce_h, ce),
        load(6, agg_h, agg),
        load(7, map_h, gm_s),
        load(8, gmv_h, gm_v),
        load(9, qk_h, qk),
        load(10, gbias_h, gbias),
        load(11, gain_h, gain),
        load(12, hbias_h, hbias),
    ]
    heads = load(13, head_h, hraw)

    def place(t, row):
        return ((yhi + row) % 2) * 4 + (x + way * ((3 * t * t - 5 * t) // 2) + 8) % 4

    swapped = {1: 1, 2: 4, 3: 5, 4: 2, 5: 3, 6: 6, 7: 7}

    def half(step):
        return wg.at[place(step // 2, step % 2), core]

    def pass_on(step, to, loc):
        rdma(half(step), half(step), esem.at[0], rsem.at[to], at(ci, loc)).start()

    def to_partner(step):
        rdma(half(step), half(step), esem.at[0], psem.at[swapped[step]], at(partner)).start()

    def arrived(step):
        await_bytes(half(step), rsem.at[step])

    first_half.wait()
    other_half.wait()
    for copy in loads:
        copy.wait()

    base = ci * BUNDLE
    groups = [gm_s[base + k] for k in range(BUNDLE)]
    low = jnp.minimum(jnp.minimum(groups[0], groups[1]), jnp.minimum(groups[2], groups[3]))
    weights = []
    for k in range(BUNDLE):
        full = 0.5 * agg[k]
        second = jnp.where(groups[k] != low, full, 0.0)
        weights.append((full - second, second))

    acc[...] = jnp.zeros_like(acc)
    tokf[...] = token[...].astype(F32)

    @pl.loop(0, BUNDLE)
    def _(c):
        hid = jnp.broadcast_to(maskv[pl.ds(c, 1), :].astype(F32), (128, LOCS)).T
        rows = pl.ds(pl.multiple_of(c * LOCS, LOCS), LOCS)
        at_lane = lax.broadcasted_iota(jnp.int32, (LOCS, 128), 1)
        px[rows, BLOCK:] = jnp.where(at_lane == 0, hid, jnp.where(at_lane == 1 + c, 1.0, 0.0)).astype(BF)
        keep[c] = 1.0 - hid

    @pl.loop(0, LOCS // 32)
    def _(i):
        rows = pl.ds(pl.multiple_of(i * 32, 32), 32)
        turned = jnp.swapaxes(raw[rows], 0, 1)
        for c in range(BUNDLE):
            shown = keep[c, rows, :]
            kept = turned[c].astype(F32) * jnp.concatenate([shown, shown], axis=1)
            px[pl.ds(pl.multiple_of(c * LOCS + i * 32, 32), 32), 0:BLOCK] = kept.astype(BF)

    @pl.loop(0, 8)
    def _(step):
        p = lax.broadcasted_iota(jnp.int32, (BLOCK, BLOCK), 0) % H
        head = 2 * step + lax.broadcasted_iota(jnp.int32, (BLOCK, BLOCK), 1) // 128
        expand[step] = jnp.where(p == head, 1.0, 0.0).astype(BF)

    row16 = lax.broadcasted_iota(jnp.int32, (128, BLOCK), 0)

    def embed_block(j):
        columns = pl.ds(pl.multiple_of(j * BLOCK, BLOCK), BLOCK)
        hide = jnp.concatenate([tokf[pl.ds(2 * j, 1), :], tokf[pl.ds(2 * j + 1, 1), :]], axis=1)
        extra = jnp.where(row16 == 0, hide, 0.0)
        embeds = ce[:, columns].astype(F32)
        for k in range(BUNDLE):
            extra = jnp.where(row16 == 1 + k, embeds[k : k + 1], extra)
        weight = jnp.concatenate([wg[j].reshape(BLOCK, BLOCK), extra.astype(BF)], axis=0)
        pre[...] = jnp.dot(px[...], weight, preferred_element_type=F32)

        @pl.loop(0, LOCS // 32, unroll=True)
        def _(chunk):
            first, second = None, None
            for k in range(BUNDLE):
                v = pre[pl.ds(pl.multiple_of(k * LOCS + chunk * 32, 32), 32), :]
                g = v + v * lax.erf(v * (1.0 / math.sqrt(2.0)))
                w0, w1 = weights[k]
                first = g * w0 if first is None else first + g * w0
                second = g * w1 if second is None else second + g * w1
            b[j, pl.ds(pl.multiple_of(chunk * 32, 32), 32), :] = first.astype(BF)
            b[j, pl.ds(pl.multiple_of(LOCS + chunk * 32, 32), 32), :] = second.astype(BF)

        q = jnp.concatenate([qk[:, columns]] * 8, axis=0)
        acc[...] += lax.dot_general(b[j], q, (((1,), (1,)), ((), ())), preferred_element_type=F32)

    embed_block(li)
    pl.semaphore_wait(barrier, CHAN - 1 + 5)
    mine = wg.at[li, core]
    rdma(mine, mine, esem.at[0], rsem.at[2], at(ci, nxt)).start()
    rdma(mine, mine, esem.at[0], rsem.at[4], at(ci, prv)).start()
    rdma(mine, mine, esem.at[0], rsem.at[1], at(ypartner, cross_loc)).start()
    rdma(mine, mine, esem.at[0], rsem.at[3], at(ypartner, diagonals[0])).start()

    @pl.loop(1, 8)
    def _(step):
        @pl.when(step == 1)
        def _():
            arrived(2)
            pass_on(2, 6, nxt)
            to_partner(2)
            arrived(4)
            to_partner(4)
            rdma(mine, mine, esem.at[0], rsem.at[5], at(ypartner, diagonals[1])).start()

        @pl.when(step == 2)
        def _():
            arrived(1)
            to_partner(1)

        @pl.when(step == 3)
        def _():
            arrived(3)
            pass_on(3, 7, nxt)
            to_partner(3)
            arrived(6)
            to_partner(6)

        @pl.when(step == 4)
        def _():
            arrived(5)
            to_partner(5)

        @pl.when(step == 6)
        def _():
            arrived(7)
            to_partner(7)

        third = ((step // 3) % 2) * (1 - (step % 3 + 1) // 2)
        fourth = (step // 4) * (1 - (step % 4 + 3) // 4)
        turn = step + third - fourth
        t, row = turn % 4, turn // 4
        j = place(t, row)
        await_bytes(wg.at[j, 1 - core], psem.at[2 * t + row])
        embed_block(j)

    lane = lax.broadcasted_iota(jnp.int32, (CHAN, 128), 1)
    part = jnp.zeros((CHAN, 128), F32)
    for q in range(8):
        part = part + jnp.where(lane // H == q, acc[q * 64 : (q + 1) * 64, :], 0.0)
    sbuf[:, 0, :] = part
    sbuf[:, 1, :] = jnp.concatenate([part[16:32], part[0:16], part[48:64], part[32:48]], axis=0)

    for_peers(lambda p: rdma(sbuf.at[p], rbuf.at[ci], ssem.at[0], srsem.at[0], at(p)).start())

    rbuf[ci] = sbuf[ci]
    gmap = jnp.broadcast_to(gm_v[...].astype(F32), (8, C))
    wide = lax.broadcasted_iota(jnp.int32, (CHAN, C), 1)
    bund = lax.broadcasted_iota(jnp.int32, (CHAN, C), 0)
    inside = wide // BUNDLE == bund
    lows = jnp.min(jnp.where(inside, gmap[0:1], 1e9), axis=1, keepdims=True)
    highs = jnp.max(jnp.where(inside, gmap[0:1], -1.0), axis=1, keepdims=True)
    gcol = lax.broadcasted_iota(jnp.int32, (CHAN, G), 1).astype(F32)
    from_group = [jnp.where(v == gcol, 1.0, 0.0).astype(BF) for v in (lows, highs)]
    to_group = [f.astype(F32).T.astype(BF) for f in from_group]

    bias = jnp.concatenate([gbias[...]] * 8, axis=0).T
    heads.wait()

    @pl.loop(0, E // 32)
    def _(i):
        rows = pl.ds(pl.multiple_of(i * 32, 32), 32)
        wd[:, rows, :] = jnp.swapaxes(hraw[rows], 0, 1)

    await_bytes(rbuf.at[pl.ds(0, CHAN - 1)], srsem.at[0])
    lane2 = lax.broadcasted_iota(jnp.int32, (CHAN, 256), 1) % 128
    got = jnp.concatenate([rbuf[:, 0, :], rbuf[:, 1, :]], axis=1)
    mixed = jnp.where(lane2 < 64, exact_dot(to_group[0], got), exact_dot(to_group[1], got))
    turned = [pltpu.roll(mixed[:, k * 128 : (k + 1) * 128], 64, 1) for k in range(2)]
    scores = mixed + jnp.concatenate(turned, axis=1) + jnp.concatenate([bias, bias], axis=1)
    top = jnp.max(scores, axis=0, keepdims=True)
    raised = jnp.exp(scores - top)
    attn = raised / jnp.sum(raised, axis=0, keepdims=True)
    back = jnp.where(lane2 < 64, exact_dot(from_group[0], attn), exact_dot(from_group[1], attn))
    upper = z >= ZS // 2
    obuf[:, 0, :] = jnp.where(upper, back[:, 128:], back[:, :128])
    obuf[:, 1, :] = jnp.where(upper, back[:, :128], back[:, 128:])
    pair = ylo * ZS + (z % (ZS // 2)) * 2 + core

    for off in (12, 3, 13, 2, 14, 1, 15):
        there = ((z + off) % ZS) * 2
        for side in (1 - ylo, ylo):
            for c in range(2):
                peer = side * 2 * ZS + there + c
                rdma(obuf.at[peer], abuf.at[pair], ssem.at[1], srsem.at[1], at(peer)).start()

    for peer in ((1 - ylo) * 2 * ZS + z * 2, (1 - ylo) * 2 * ZS + z * 2 + 1, partner):
        rdma(obuf.at[peer], abuf.at[pair], ssem.at[1], srsem.at[1], at(peer)).start()

    abuf[pair] = obuf[ci]
    await_bytes(abuf.at[pl.ds(0, 31)], srsem.at[1])
    low_sets, high_sets = abuf[:, 0, :], abuf[:, 1, :]
    received = jnp.concatenate([low_sets[0:16], high_sets[0:16], low_sets[16:32], high_sets[16:32]], axis=0)
    high, rest = split(received, 2)
    high, rest = high.astype(F32), rest.astype(F32)
    for q in range(8):
        lhs[q * 64 : (q + 1) * 64, 0:128] = jnp.where(lane // H == q, high, 0.0).astype(BF)
        lhs[q * 64 : (q + 1) * 64, 128:256] = jnp.where(lane // H == q, rest, 0.0).astype(BF)

    def weigh(j):
        spread = jnp.dot(lhs[...], expand[j], preferred_element_type=F32)
        return spread[:LOCS] * b[j, 0:LOCS, :].astype(F32) + spread[LOCS:] * b[j, LOCS:, :].astype(F32)

    @pl.loop(0, 4)
    def _(t):
        ps[t] = weigh((1 - core) * 4 + t).astype(BF)
        rdma(ps.at[t], pr.at[t], csem.at[0], crsem.at[t], at(partner)).start()

    @pl.loop(0, 4)
    def _(t):
        mixed_in = weigh(core * 4 + t)
        await_bytes(pr.at[t], crsem.at[t])
        own[t] = mixed_in + pr[t].astype(F32)
        theirs = pl.ds(pl.multiple_of((1 - ylo) * 128, 128), 128)
        ys[t] = own[t, theirs, :].astype(BF)
        rdma(ys.at[t], yr.at[t], csem.at[1], yrsem.at[t], at(ypartner)).start()

    def zdev(to):
        return at(ylo * 2 * ZS + to * 2 + core)

    def ahead(n):
        return (z + way * n + ZS) % ZS

    @pl.loop(0, 4)
    def _(t):
        mine = pl.ds(pl.multiple_of(ylo * 128, 128), 128)
        await_bytes(yr.at[t], yrsem.at[t])
        total = own[t, mine, :] + yr[t].astype(F32)
        total = total.reshape(ZS, 8, BLOCK)
        zf[t] = total
        zs[t] = total.astype(BF)
        for d in (8, 7, 6, 5):
            to, via = ahead(d), ahead(d - 4)
            rdma(zs.at[t, to], rin.at[t, 0, d - 5], zsem.at[0], rinsem.at[0, t], zdev(via)).start()
            if d < 8:
                to, via = ahead(-d), ahead(4 - d)
                rdma(zs.at[t, to], rin.at[t, 1, d - 5], zsem.at[0], rinsem.at[1, t], zdev(via)).start()
        for d in (3, 2, 1):
            for q, to in enumerate((ahead(d), ahead(-d))):
                rdma(zs.at[t, to], zr.at[t, q, d - 1], zsem.at[0], zrsem.at[t], zdev(to)).start()

    @pl.loop(0, 4)
    def _(t):
        for q, to, n in ((0, ahead(4), 4), (1, ahead(-4), 3)):
            await_bytes(rin.at[t, q, pl.ds(0, n)], rinsem.at[q, t])
            total = zf[t, to]
            for d in range(n):
                total = total + rin[t, q, d].astype(F32)
            rout[t, q] = total.astype(BF)
            rdma(rout.at[t, q], zr.at[t, q, 3], zsem.at[1], zrsem.at[t], zdev(to)).start()

    squares = jnp.zeros((8, 1), F32)
    for t in range(4):
        await_bytes(zr.at[t], zrsem.at[t])
        total = zf[t, z]
        for q in range(2):
            for d in range(4):
                total = total + zr[t, q, d].astype(F32)
        pooled[:, t * BLOCK : (t + 1) * BLOCK] = total
        squares = squares + jnp.sum(total * total, axis=1, keepdims=True)
    ssb[...] = jnp.broadcast_to(squares, (8, 128))
    share = rdma(ssb, ssr, csem.at[3], qrsem.at[0], at(partner))
    share.start()
    scaled = pooled[...] * gain[:, pl.ds(pl.multiple_of(core * 1024, 1024), 1024)]
    share.wait_recv()
    inverse = lax.rsqrt((squares + ssr[:, 0:1]) * (1.0 / E) + 1e-06)
    jt[core, ylo, z] = (scaled * inverse).astype(BF)

    def row_block(row, d):
        return jt.at[core, row, ahead(-d)]

    def spread(d, way_z, steps):
        for n in steps:
            block = row_block(ylo, d)
            there = (d + way_z * n) % ZS
            rdma(block, block, jsem.at[0], jz.at[there], zdev(ahead(way_z * n))).start()

    def share_block(d):
        block = row_block(ylo, d)
        rdma(block, block, jsem.at[1], jy.at[d], at(ypartner)).start()
        rdma(block, block, jsem.at[2], jc.at[d], at(partner)).start()

    for n in (4, 3, 2, 1):
        spread(0, 1, (n,))
        spread(0, -1, (n,))
    share_block(0)
    order = (1, 15, 4, 12, 2, 14, 3, 13, 5, 11, 6, 10, 7, 9, 8)
    for d in order:
        await_bytes(row_block(ylo, d), jz.at[d])
        if d == 4:
            spread(4, 1, (4, 3, 2, 1))
        if d == 12:
            spread(12, -1, (3, 2, 1))
        share_block(d)
    def decode_own(row):
        side = jt[core, row].reshape(128, 1024)

        @pl.loop(0, BUNDLE, unroll=True)
        def _(c):
            part = wd[c, pl.ds(pl.multiple_of(core * 1024, 1024), 1024), :]
            dec[c] = jnp.dot(side, part, preferred_element_type=F32) + hbias[pl.ds(c, 1), :]

    def decode_rest(row):
        side = jt[1 - core, row].reshape(128, 1024)

        @pl.loop(0, BUNDLE, unroll=True)
        def _(c):
            part = wd[c, pl.ds(pl.multiple_of((1 - core) * 1024, 1024), 1024), :]
            rows = pl.ds(pl.multiple_of(row * 128, 128), 128)
            columns = pl.ds(pl.multiple_of(c * BLOCK, BLOCK), BLOCK)
            out[rows, columns] = (dec[c] + jnp.dot(side, part, preferred_element_type=F32)).astype(BF)

    decode_own(ylo)
    for d in range(ZS):
        await_bytes(jt.at[1 - core, ylo, ahead(d)], jc.at[d])
    decode_rest(ylo)
    for d in (0, *order):
        block = row_block(1 - ylo, d)
        await_bytes(block, jy.at[d])
        rdma(block, block, jsem.at[2], jd.at[d], at(partner)).start()
    decode_own(1 - ylo)
    for d in range(ZS):
        await_bytes(jt.at[1 - core, 1 - ylo, ahead(d)], jd.at[d])
    decode_rest(1 - ylo)

    await_bytes(wg.at[pl.ds(0, 7)], esem.at[0])
    await_bytes(sbuf.at[pl.ds(0, CHAN - 1)], ssem.at[0])
    await_bytes(obuf.at[pl.ds(0, 31)], ssem.at[1])
    await_bytes(ps, csem.at[0])
    await_bytes(ys, csem.at[1])
    await_bytes(zs.at[:, pl.ds(0, 13)], zsem.at[0])
    await_bytes(rout, zsem.at[1])
    share.wait_send()
    await_bytes(jt.at[0, 0, pl.ds(0, ZS - 1)], jsem.at[0])
    await_bytes(jt.at[0, 0], jsem.at[1])
    await_bytes(jt.at[0], jsem.at[2])


def shards(
    pixels,
    patch_mask,
    group_map,
    embed_weight,
    mask_token,
    chan_embed,
    agg_weight,
    query_key,
    group_bias,
    norm_gain,
    head_weight,
    head_bias,
):
    vmem = pl.BlockSpec(memory_space=pltpu.VMEM)
    hbm = pl.BlockSpec(memory_space=pltpu.HBM)
    dma = pltpu.SemaphoreType.DMA
    decoded = pl.pallas_call(
        kernel,
        out_shape=jax.ShapeDtypeStruct((LOCS, BUNDLE * BLOCK), BF),
        in_specs=[hbm] * 13,
        out_specs=vmem,
        scratch_shapes=[
            pltpu.VMEM((LOCS, BUNDLE, BLOCK), BF),
            pltpu.VMEM((BUNDLE, LOCS), jnp.int32),
            pltpu.VMEM((16, 128), BF),
            pltpu.VMEM((BUNDLE, E), BF),
            pltpu.SMEM((BUNDLE,), F32),
            pltpu.SMEM((C,), jnp.int32),
            pltpu.VMEM((1, C), jnp.int32),
            pltpu.VMEM((H, E), BF),
            pltpu.VMEM((H, G), F32),
            pltpu.VMEM((1, E), F32),
            pltpu.VMEM((E, BUNDLE, BLOCK), BF),
            pltpu.VMEM((BUNDLE, BLOCK), F32),
            pltpu.VMEM((16, 128), F32),
            pltpu.VMEM((BUNDLE, LOCS, 128), F32),
            pltpu.VMEM((BUNDLE * LOCS, BLOCK + 128), BF),
            pltpu.VMEM((BUNDLE, E, BLOCK), BF),
            pltpu.VMEM((BUNDLE, 128, BLOCK), F32),
            pltpu.VMEM((8, 2, 128, BLOCK), BF),
            pltpu.VMEM((8, 2 * LOCS, BLOCK), BF),
            pltpu.VMEM((BUNDLE * LOCS, BLOCK), F32),
            pltpu.VMEM((2 * LOCS, 128), F32),
            pltpu.VMEM((8, BLOCK, BLOCK), BF),
            pltpu.VMEM((CHAN, 2, 128), F32),
            pltpu.VMEM((CHAN, 2, 128), F32),
            pltpu.VMEM((CHAN, 2, 128), F32),
            pltpu.VMEM((CHAN // 2, 2, 128), F32),
            pltpu.VMEM((2 * LOCS, 256), BF),
            pltpu.VMEM((4, LOCS, BLOCK), BF),
            pltpu.VMEM((4, LOCS, BLOCK), BF),
            pltpu.VMEM((4, LOCS, BLOCK), F32),
            pltpu.VMEM((4, 128, BLOCK), BF),
            pltpu.VMEM((4, 128, BLOCK), BF),
            pltpu.VMEM((4, ZS, 8, BLOCK), BF),
            pltpu.VMEM((4, ZS, 8, BLOCK), F32),
            pltpu.VMEM((4, 2, 4, 8, BLOCK), BF),
            pltpu.VMEM((4, 2, 4, 8, BLOCK), BF),
            pltpu.VMEM((4, 2, 8, BLOCK), BF),
            pltpu.VMEM((8, 1024), F32),
            pltpu.VMEM((8, 128), F32),
            pltpu.VMEM((8, 128), F32),
            pltpu.VMEM((2, 2, ZS, 8, 1024), BF),
            dma((14,)),
            dma((1,)),
            dma((8,)),
            dma((8,)),
            dma((2,)),
            dma((2,)),
            dma((4,)),
            dma((4,)),
            dma((4,)),
            dma((2,)),
            dma((2, 4)),
            dma((4,)),
            dma((1,)),
            dma((3,)),
            dma((ZS,)),
            dma((ZS,)),
            dma((ZS,)),
            dma((ZS,)),
        ],
        compiler_params=pltpu.CompilerParams(
            collective_id=0, has_side_effects=True, vmem_limit_bytes=32 * 1024 * 1024
        ),
    )(*[pltpu.with_memory_space_constraint(v, pltpu.HBM) for v in (
        pixels,
        patch_mask.T,
        embed_weight,
        mask_token.reshape(16, 128),
        chan_embed,
        agg_weight,
        group_map,
        group_map.reshape(1, C),
        query_key,
        group_bias,
        norm_gain.reshape(1, E),
        head_weight,
        head_bias,
    )])
    return decoded.reshape(pixels.shape)


def solution(mesh):
    return jax.shard_map(
        shards,
        mesh=mesh,
        in_specs=(
            P("loc", "chan", None),
            P("loc", "chan"),
            P(),
            P(None, "loc"),
            P(),
            P("chan", None),
            P("chan"),
            P(),
            P(),
            P(),
            P(None, "chan", None),
            P("chan", None),
        ),
        out_specs=P("loc", "chan", None),
        check_vma=False,
    )
```
